256 devices in a mesh: corpus: 8 (over z), cent: 32 (over x, y, core).
Axes of the slice: x: 4, y: 4, z: 8, core: 2. Of those that a mesh axis runs over, the one named last changes fastest.
Arguments:
- queries: bfloat16 [8, 32, 32, 128], P('corpus', 'cent'), may hold values from -0.5 to 0.5
- candidates: int32 [8, 8, 32, 32], P('corpus', None, 'cent'), may hold values from 0 to 2047, as said below
- storage_row: int32 [8, 2048], P('corpus'), may hold values from 0 to 2047, as said below
- lengths: int32 [8, 2048], P('corpus', 'cent'), may hold values from 8 to 128, as said below
- token_cents: int32 [8, 2048, 128], P('corpus', 'cent'), may hold values from 0 to 262143, as said below
- residual_codes: int32 [8, 2048, 128, 128], P('corpus', 'cent'), may hold values from 0 to 3
- centroids: bfloat16 [262144, 128], P('cent'), may hold values from -0.5 to 0.5
- bucket_weights: float32 [4], replicated, may hold values from -0.3 to 0.3
Outputs:
- scores: float32 [8, 32, 256], P('corpus', 'cent')
The draws below stay inside these ranges and needn't reach their ends.
Inputs may be any that keep to these rules, and one draw needn't show every extreme that they name: `storage_row`: for each shard, a permutation of the storage rows; row r is stored on cent index r // 64. `candidates`: ids of shard g; of all candidate entries held by one device, at most 16 name passages stored on any one cent index, and in each shard one cent index receives exactly 16 of them from every device of the group. `lengths`: the first storage row of every device holds a passage of 128 tokens. `token_cents`: the token slots of rows stored on cent index j hold ids from j * 8192 to (j + 1) * 8192 - 1.
All inputs are finite; a program needn't handle non-finite values.
Results may differ from the reference program's by a relative error of at most 0.0003.
Values may be sent and summed in bfloat16 or wider, within the bound.
A program may use at most 128 MiB of HBM per device.

```python
import jax
import jax.numpy as jnp
from jax import lax

DIM = 128
QT = 32
PT = 128
BUCKETS = 4
Q_DEV = 1
K_SHARD = 32
P_DEV = 64
CENT_DEV = 8192
P_GROUP = 2048
QB = 32
NCENT = 262144
CAP = 16
N_CORPUS = 8
N_CENT = 32


def storage_table(key):
    base = jax.random.fold_in(key, 11)
    shard_keys = jax.random.split(base, N_CORPUS)

    def one_shard(shard_key):
        return jax.random.permutation(shard_key, P_GROUP).astype(jnp.int32)
    return jax.vmap(one_shard)(shard_keys)


def draw_storage_row(key, part):
    return storage_table(key)


def draw_candidates(key, part):
    table = storage_table(key)
    counting = jnp.arange(P_GROUP, dtype=jnp.int32)

    def invert(row_table):
        return jnp.zeros((P_GROUP,), jnp.int32).at[row_table].set(counting)
    inverse = jax.vmap(invert)(table)
    total = N_CORPUS * Q_DEV * K_SHARD
    slots = N_CENT * CAP
    base = jax.random.fold_in(key, 23)
    hottest = jax.random.randint(jax.random.fold_in(base, 1), (N_CORPUS,), 0, N_CENT).astype(jnp.int32)

    def one_member(shard, member):
        member_key = jax.random.fold_in(jax.random.fold_in(jax.random.fold_in(base, 2), shard), member)
        first_key, second_key, third_key = jax.random.split(member_key, 3)
        order = jax.random.permutation(first_key, slots).astype(jnp.int32)
        ranking = jnp.where(order // CAP == hottest[shard], 0, slots) + jnp.arange(slots, dtype=jnp.int32)
        ordered = order[jnp.argsort(ranking, stable=True)]
        owners = ordered[:total] // CAP
        owners = owners[jax.random.permutation(second_key, total)]
        within = jax.random.randint(third_key, (total,), 0, P_DEV).astype(jnp.int32)
        rows = owners * P_DEV + within
        return inverse[shard][rows].reshape(N_CORPUS, Q_DEV, K_SHARD)
    shards = jnp.arange(N_CORPUS, dtype=jnp.int32)
    members = jnp.arange(N_CENT, dtype=jnp.int32)
    grid = jax.vmap(lambda shard: jax.vmap(lambda member: one_member(shard, member))(members))(shards)
    grid = jnp.transpose(grid, (0, 2, 1, 3, 4))
    return grid.reshape(N_CORPUS, N_CORPUS, QB, K_SHARD).astype(jnp.int32)


def draw_lengths(key, part):
    counts = jax.random.randint(jax.random.fold_in(key, 31), (N_CORPUS, P_GROUP), 8, PT + 1).astype(jnp.int32)
    return counts.at[:, ::P_DEV].set(PT)


def draw_token_cents(key, part):
    local_ids = jax.random.randint(jax.random.fold_in(key, 41), (N_CORPUS, P_GROUP, PT), 0, CENT_DEV).astype(jnp.int32)
    offsets = jnp.arange(P_GROUP, dtype=jnp.int32) // P_DEV * CENT_DEV
    return local_ids + offsets[None, :, None]


def set_ends(result, stream_key, least, top_value):
    dims = result.shape
    index_at = [jax.random.randint(jax.random.fold_in(stream_key, axis), (), 0, dims[axis]) for axis in range(len(dims))]
    result = result.at[tuple(index_at)].set(least)
    longest = dims.index(max(dims))
    index_at[longest] = (index_at[longest] + 1) % dims[longest]
    return result.at[tuple(index_at)].set(top_value)


def steps_of(stream_key, dims, pieces, least, largest):
    factor_of, own = 1.0, jax.random.fold_in(stream_key, 6)
    for dim, parts in pieces:
        draws = jnp.exp(jax.random.uniform(jax.random.fold_in(own, dim), (parts,), jnp.float32, least / len(pieces), largest / len(pieces)))
        factor_of = factor_of * jnp.repeat(draws, dims[dim] // parts).reshape([-1 if axis == dim else 1 for axis in range(len(dims))])
    return factor_of


def normal_values(own_key, shape, width, most, pieces=(), kind=jnp.bfloat16):
    factor_of = steps_of(own_key, shape, pieces, -0.22, 0.18) if pieces else 1.0
    drawn = jax.random.normal(own_key, shape, jnp.float32) * width * factor_of
    return jnp.minimum(jnp.maximum(drawn, -most), most).astype(kind)


def setup_inputs(seed: int = 0) -> dict:
    key_list = jax.random.split(jax.random.key(seed), 9)
    return {
        "queries": normal_values(key_list[0], (N_CORPUS, QB, QT, DIM), 0.09, 0.5, ((0, 8), (1, 32))),
        "candidates": draw_candidates(jax.random.fold_in(key_list[8], 71), 0),
        "storage_row": draw_storage_row(jax.random.fold_in(key_list[8], 71), 0),
        "lengths": draw_lengths(jax.random.fold_in(key_list[8], 71), 0),
        "token_cents": draw_token_cents(jax.random.fold_in(key_list[8], 71), 0),
        "residual_codes": set_ends(jax.random.randint(key_list[5], (N_CORPUS, P_GROUP, PT, DIM), 0, BUCKETS), jax.random.fold_in(key_list[5], 1), 0, BUCKETS - 1).astype(jnp.int32),
        "centroids": normal_values(key_list[6], (NCENT, DIM), DIM ** -0.5, 0.5, ((0, 32),)),
        "bucket_weights": normal_values(key_list[7], (BUCKETS,), 0.06, 0.3, (), jnp.float32),
    }


def pick_bucket(code_values, bucket_weights):
    picked = jnp.zeros(code_values.shape, jnp.float32)
    for level in range(bucket_weights.shape[0]):
        picked = picked + jnp.where(code_values == level, bucket_weights[level], jnp.float32(0.0))
    return picked

def decompress(centroid_rows, token_ids, code_values, bucket_weights):
    base = jnp.take(centroid_rows, token_ids, axis=0).astype(jnp.float32)
    summed = base + pick_bucket(code_values, bucket_weights)
    factor = lax.rsqrt(lax.optimization_barrier(jnp.sum(summed * summed, axis=-1, keepdims=True)) + 1e-06)
    return (summed * factor).astype(jnp.bfloat16)

def masked_sum(dots, counts):
    slots = jnp.arange(dots.shape[-1], dtype=jnp.float32)
    valid = slots < counts[..., None, None]
    best = lax.optimization_barrier(jnp.max(jnp.where(valid, dots, jnp.float32(-1e+30)), axis=-1))
    return lax.optimization_barrier(jnp.sum(best, axis=-1))

def reference(queries, candidates, storage_row, lengths, token_cents, residual_codes, centroids, bucket_weights):

    def shard_scores(shard):
        rows_all = jnp.take(storage_row[shard], candidates[shard], axis=0)
        cents = token_cents[shard]
        codes_here = residual_codes[shard]
        counts_here = lengths[shard]

        def owner_scores(group):
            rows = rows_all[group].reshape(-1)
            embed = decompress(centroids, jnp.take(cents, rows, axis=0), jnp.take(codes_here, rows, axis=0), bucket_weights)
            embed = embed.reshape(QB, K_SHARD, PT, DIM).astype(jnp.float32)
            query = queries[group].astype(jnp.float32)
            dots = jnp.einsum('atd,aksd->akts', query, embed)
            counts = jnp.take(counts_here, rows, axis=0).reshape(QB, K_SHARD).astype(jnp.float32)
            return masked_sum(dots, counts)
        return lax.map(owner_scores, jnp.arange(N_CORPUS, dtype=jnp.int32))
    every = lax.map(shard_scores, jnp.arange(N_CORPUS, dtype=jnp.int32))
    return jnp.transpose(every, (1, 2, 0, 3)).reshape(N_CORPUS, QB, N_CORPUS * K_SHARD)
```

```python
import jax
import jax.numpy as jnp
from jax import lax
from jax.experimental import pallas as pl
from jax.experimental.pallas import tpu as pltpu
from jax.sharding import PartitionSpec as P

DIM = 128
QT = 32
PT = 128
GROUPS = 8
MEMBERS = 32
K = 32
ENTRIES = 256
CAP = 16
SLOTS = MEMBERS * CAP
PASSAGES = 64
CENTS = 8192
WIDE = 8
CHUNKS = 120
EARLY = 16
MESH = pl.DeviceIdType.MESH
HIGH = lax.Precision.HIGHEST
NT = (((1,), (1,)), ((), ()))
F32, I32, BF16 = jnp.float32, jnp.int32, jnp.bfloat16


def iota(shape, dim):
    return lax.broadcasted_iota(I32, shape, dim)


def one_hot(flag):
    return jnp.where(flag, F32(1.0), F32(0.0))


def dot(a, b):
    return jnp.dot(a, b, preferred_element_type=F32)


def request_tiles(cand, table, member):
    lanes = iota((32, ENTRIES), 1)
    spread = one_hot(lanes % K == iota((32, ENTRIES), 0))
    wide = jnp.dot(cand.astype(F32), spread, precision=HIGH, preferred_element_type=F32)
    mine = iota((GROUPS, ENTRIES), 1) // K == iota((GROUPS, ENTRIES), 0)
    ident = jnp.sum(jnp.where(mine, wide, 0.0), axis=0, keepdims=True).astype(I32)
    low = one_hot(iota((128, ENTRIES), 0) == (ident & 127))
    looked = jnp.dot(table.astype(F32), low, precision=HIGH, preferred_element_type=F32)
    high = iota((16, ENTRIES), 0) == (ident >> 7)
    row = jnp.sum(jnp.where(high, looked, 0.0), axis=0, keepdims=True).astype(I32)
    owner, stored = row >> 6, row & 63
    owned = one_hot(iota((MEMBERS, ENTRIES), 0) == owner)
    before = one_hot(iota((ENTRIES, ENTRIES), 0) < iota((ENTRIES, ENTRIES), 1))
    ahead = dot(owned.astype(BF16), before.astype(BF16))
    position = jnp.sum(owned * ahead, axis=0, keepdims=True).astype(I32)
    code = (stored * ENTRIES + iota((1, ENTRIES), 1) + 1).astype(F32)
    place = one_hot(iota((128, ENTRIES), 0) == position + (member % 8) * CAP)
    tiles = lax.dot_general(
        owned * code, place, NT, precision=HIGH, preferred_element_type=F32
    )
    return tiles.astype(I32)


def chunk_tables(packed):
    code = jnp.concatenate([packed[r : r + 1, :] for r in range(4)], axis=1)
    there = code > 0
    stored = jnp.where(there, (code - 1) >> 8, PASSAGES)
    entry = jnp.where(there, (code - 1) & 255, 0)
    group, cand = entry >> 5, entry & 31
    source = iota((1, SLOTS), 1) >> 4
    named = one_hot(iota((PASSAGES, SLOTS), 0) == stored)
    namedb = named.astype(BF16)
    before = one_hot(iota((SLOTS, SLOTS), 0) < iota((SLOTS, SLOTS), 1)).astype(BF16)
    ahead = dot(namedb, before)
    position = jnp.sum(named * ahead, axis=0, keepdims=True).astype(I32)
    count = dot(namedb, jnp.ones((SLOTS, 128), BF16)).astype(I32)
    needed = (count + (WIDE - 1)) >> 3
    lower = one_hot(iota((PASSAGES, PASSAGES), 1) < iota((PASSAGES, PASSAGES), 0))
    first = dot(lower.astype(BF16), needed.astype(F32).astype(BF16))
    first4 = jnp.concatenate([first] * 4, axis=1)
    chunk = jnp.sum(named * first4, axis=0, keepdims=True).astype(I32) + (position >> 3)
    in_chunk = one_hot((iota((128, SLOTS), 0) == chunk) & there).astype(BF16)
    column = iota((WIDE, SLOTS), 0) == (position & 7)

    def placed(value):
        return jnp.where(column, value.astype(F32), 0.0)

    values = jnp.concatenate(
        [
            placed(source * GROUPS + group),
            placed(source * 2 + (group >> 2) + 1),
            placed((group & 3) * K + cand),
        ],
        axis=0,
    ).astype(BF16)
    tables = lax.dot_general(values, in_chunk, NT, preferred_element_type=F32).astype(I32)
    ends = first.astype(I32) + needed
    passed = jnp.where(ends <= iota((PASSAGES, 128), 1), 1.0, 0.0)
    passage = jnp.sum(passed, axis=0, keepdims=True).astype(I32)
    passage = jnp.minimum(passage, PASSAGES - 1)
    index = jnp.concatenate(
        [tables[0:WIDE], jnp.broadcast_to(passage, (8, 128))], axis=0
    )
    return index, tables[8:16], tables[16:24]


def kernel(
    q_ref,
    cand_ref,
    table_ref,
    len_ref,
    tok_ref,
    codes_hbm,
    cent_hbm,
    bw_ref,
    out_ref,
    codes,
    cent,
    table32,
    rows,
    embed,
    queries,
    asks,
    asked,
    index_v,
    index_s,
    slot_row,
    slot_lane,
    best,
    part,
    parts,
    last,
    lasts,
    code_sem,
    cent_sem,
    local_sem,
    z_send,
    z_recv,
    ask_send,
    ask_recv,
    q_send,
    q_recv,
    fwd_send,
    part_send,
    part_recv,
    last_send,
    last_recv,
):
    shard = lax.axis_index("corpus")
    member = lax.axis_index("cent")
    core = member % 2
    chip = member // 2
    partner = chip * 2 + (1 - core)

    def peer(step):
        return lax.rem(member + step, MEMBERS)

    def other(step):
        return lax.rem(shard + step, GROUPS)

    def code_copy(p):
        return pltpu.make_async_copy(codes_hbm.at[p], codes.at[p], code_sem.at[p])

    cent_copy = pltpu.make_async_copy(cent_hbm, cent, cent_sem)
    cent_copy.start()
    own_query = pltpu.make_async_copy(
        q_ref, queries.at[member * GROUPS + shard], local_sem.at[0]
    )
    own_query.start()

    barrier = pltpu.get_barrier_semaphore()
    for step in range(1, MEMBERS):
        pl.semaphore_signal(
            barrier, inc=1, device_id=(shard, peer(step)), device_id_type=MESH
        )
    for step in range(1, GROUPS):
        pl.semaphore_signal(
            barrier, inc=1, device_id=(other(step), member), device_id_type=MESH
        )

    def start_codes(p, carry):
        code_copy(p).start()
        return carry

    lax.fori_loop(0, PASSAGES, start_codes, 0)

    tiles = request_tiles(cand_ref[...], table_ref[...], member)
    row = iota((8, 128), 0) == member // 8
    for m in range(MEMBERS):
        asks[m] = jnp.where(row, jnp.broadcast_to(tiles[m : m + 1, :], (8, 128)), 0)

    pl.semaphore_wait(barrier, MEMBERS + GROUPS - 2)

    def z_copy(step):
        return pltpu.make_async_remote_copy(
            src_ref=q_ref,
            dst_ref=queries.at[member * GROUPS + shard],
            send_sem=z_send.at[step - 1],
            recv_sem=z_recv.at[step - 1],
            device_id=(other(step), member),
            device_id_type=MESH,
        )

    def ask_copy(step):
        return pltpu.make_async_remote_copy(
            src_ref=asks.at[peer(step)],
            dst_ref=asked.at[member],
            send_sem=ask_send.at[step - 1],
            recv_sem=ask_recv.at[step - 1],
            device_id=(shard, peer(step)),
            device_id_type=MESH,
        )

    for step in range(1, GROUPS):
        z_copy(step).start()
    for step in range(1, MEMBERS):
        ask_copy(step).start()
    own_ask = pltpu.make_async_copy(asks.at[member], asked.at[member], local_sem.at[1])
    own_ask.start()

    cent_copy.wait()

    def widen(i, carry):
        s = pl.ds(pl.multiple_of(i * 256, 256), 256)
        table32[s, :] = cent[s, :].astype(F32)
        return carry

    lax.fori_loop(0, CENTS // 256, widen, 0)
    w0, w1, w2, w3 = bw_ref[0], bw_ref[1], bw_ref[2], bw_ref[3]

    def decode(p, carry):
        code_copy(p).wait()
        for s in range(PT):
            i = tok_ref[p, s] & (CENTS - 1)
            rows[pl.ds(s, 1), :] = table32[pl.ds(i, 1), :]
        length = len_ref[0, p]
        top = None
        for s0 in range(0, PT, 32):
            c = codes[p, pl.ds(s0, 32), :]
            r = jnp.where(
                c < 2, jnp.where(c == 0, w0, w1), jnp.where(c == 2, w2, w3)
            )
            x = rows[pl.ds(s0, 32), :] + r
            y = x * lax.rsqrt(jnp.sum(x * x, axis=-1, keepdims=True) + 1e-6)
            if s0 == 0:
                top = jnp.broadcast_to(y[0:1, :], (32, DIM))
            y = jnp.where(iota((32, DIM), 0) + s0 < length, y, top)
            embed[p, pl.ds(s0, 32), :] = y.astype(BF16)
        return carry

    lax.fori_loop(0, EARLY, decode, 0)

    own_query.wait()
    for step in range(1, GROUPS):
        z_copy(step).wait()

    mine = pl.ds(member * GROUPS, GROUPS)

    def q_copy(step):
        target = lax.rem(chip + step, MEMBERS // 2) * 2 + core
        return pltpu.make_async_remote_copy(
            src_ref=queries.at[mine],
            dst_ref=queries.at[mine],
            send_sem=q_send.at[step],
            recv_sem=q_recv.at[step],
            device_id=(shard, target),
            device_id_type=MESH,
        )

    def fwd_copy(step):
        source = lax.rem(chip + MEMBERS // 2 - step, MEMBERS // 2) * 2 + core
        block = pl.ds(source * GROUPS, GROUPS)
        return pltpu.make_async_remote_copy(
            src_ref=queries.at[block],
            dst_ref=queries.at[block],
            send_sem=fwd_send.at[step],
            recv_sem=q_recv.at[MEMBERS // 2 + step],
            device_id=(shard, partner),
            device_id_type=MESH,
        )

    for step in range(1, MEMBERS // 2):
        q_copy(step).start()
    fwd_copy(0).start()

    lax.fori_loop(EARLY, PASSAGES, decode, 0)

    own_ask.wait()
    for step in range(1, MEMBERS):
        ask_copy(step).wait()
    packed = asked[0]
    for m in range(1, MEMBERS):
        packed = packed + asked[m]
    index, srow, slane = chunk_tables(packed)
    index_v[...] = index
    slot_row[...] = srow
    slot_lane[...] = slane
    index_copy = pltpu.make_async_copy(index_v, index_s, local_sem.at[2])
    index_copy.start()
    index_copy.wait()

    for step in range(1, MEMBERS // 2):
        q_copy(step).wait()
        fwd_copy(step).start()
    for step in range(MEMBERS // 2):
        fwd_copy(step).wait()

    best[pl.ds(CHUNKS, 128 - CHUNKS), :] = jnp.zeros((128 - CHUNKS, WIDE * QT), F32)

    def score(b, carry):
        found = []
        for u in range(8):
            ch = b * 8 + u
            e = embed[index_s[8, ch] & (PASSAGES - 1)]
            q = jnp.concatenate(
                [queries[index_s[j, ch] & 255] for j in range(WIDE)], axis=0
            )
            dots = lax.dot_general(e, q, NT, preferred_element_type=F32)
            found.append(jnp.max(dots, axis=0, keepdims=True))
        best[pl.ds(pl.multiple_of(b * 8, 8), 8), :] = jnp.concatenate(found, axis=0)
        return carry

    lax.fori_loop(0, CHUNKS // 8, score, 0)

    gather = one_hot(iota((WIDE, WIDE * QT), 1) // QT == iota((WIDE, WIDE * QT), 0))
    total = lax.dot_general(
        gather, best[...], NT, precision=HIGH, preferred_element_type=F32
    )
    left, right = [], []
    for j in range(WIDE):
        at = iota((64, 128), 0) + 1 == slot_row[j : j + 1, :]
        left.append(jnp.where(at, jnp.broadcast_to(total[j : j + 1, :], (64, 128)), 0.0))
        right.append(one_hot(iota((128, 128), 0) == slot_lane[j : j + 1, :]))
    table = lax.dot_general(
        jnp.concatenate(left, axis=1),
        jnp.concatenate(right, axis=1),
        NT,
        precision=HIGH,
        preferred_element_type=F32,
    )
    for m in range(MEMBERS):
        part[m] = table[2 * m : 2 * m + 2, :]

    def part_copy(step):
        return pltpu.make_async_remote_copy(
            src_ref=part.at[peer(step)],
            dst_ref=parts.at[member],
            send_sem=part_send.at[step - 1],
            recv_sem=part_recv.at[step - 1],
            device_id=(shard, peer(step)),
            device_id_type=MESH,
        )

    for step in range(1, MEMBERS):
        part_copy(step).start()
    own_part = pltpu.make_async_copy(part.at[member], parts.at[member], local_sem.at[3])
    own_part.start()
    own_part.wait()
    for step in range(1, MEMBERS):
        part_copy(step).wait()
    tot = parts[0]
    for m in range(1, MEMBERS):
        tot = tot + parts[m]

    quarter = iota((8, 128), 1) // K == shard % 4
    row_in = iota((2, 128), 0) == shard // 4
    for o in range(GROUPS):
        line = jnp.broadcast_to(tot[o // 4 : o // 4 + 1, :], (8, 128))
        shift = lax.rem(shard + 4 - o % 4, 4) * K
        line = jnp.where(quarter, pltpu.roll(line, shift, 1), 0.0)
        last[o] = jnp.where(row_in, line[0:2, :], 0.0)

    def last_copy(step):
        return pltpu.make_async_remote_copy(
            src_ref=last.at[other(step)],
            dst_ref=lasts.at[shard],
            send_sem=last_send.at[step - 1],
            recv_sem=last_recv.at[step - 1],
            device_id=(other(step), member),
            device_id_type=MESH,
        )

    for step in range(1, GROUPS):
        last_copy(step).start()
    own_last = pltpu.make_async_copy(last.at[shard], lasts.at[shard], local_sem.at[4])
    own_last.start()
    own_last.wait()
    for step in range(1, GROUPS):
        last_copy(step).wait()
    scores = lasts[0]
    for o in range(1, GROUPS):
        scores = scores + lasts[o]
    out_ref[...] = scores


def body(
    queries,
    candidates,
    storage_row,
    lengths,
    token_cents,
    residual_codes,
    centroids,
    bucket_weights,
):
    vmem = pl.BlockSpec(memory_space=pltpu.VMEM)
    smem = pl.BlockSpec(memory_space=pltpu.SMEM)
    hbm = pl.BlockSpec(memory_space=pl.ANY)
    dma = pltpu.SemaphoreType.DMA
    out = pl.pallas_call(
        kernel,
        out_shape=jax.ShapeDtypeStruct((2, 128), F32),
        in_specs=[vmem, vmem, vmem, smem, smem, hbm, hbm, smem],
        out_specs=vmem,
        scratch_shapes=[
            pltpu.VMEM((PASSAGES, PT, DIM), I32),
            pltpu.VMEM((CENTS, DIM), BF16),
            pltpu.VMEM((CENTS, DIM), F32),
            pltpu.VMEM((PT, DIM), F32),
            pltpu.VMEM((PASSAGES, PT, DIM), BF16),
            pltpu.VMEM((MEMBERS * GROUPS, QT, DIM), BF16),
            pltpu.VMEM((MEMBERS, 8, 128), I32),
            pltpu.VMEM((MEMBERS, 8, 128), I32),
            pltpu.VMEM((16, 128), I32),
            pltpu.SMEM((16, 128), I32),
            pltpu.VMEM((8, 128), I32),
            pltpu.VMEM((8, 128), I32),
            pltpu.VMEM((128, WIDE * QT), F32),
            pltpu.VMEM((MEMBERS, 2, 128), F32),
            pltpu.VMEM((MEMBERS, 2, 128), F32),
            pltpu.VMEM((GROUPS, 2, 128), F32),
            pltpu.VMEM((GROUPS, 2, 128), F32),
            dma((PASSAGES,)),
            dma,
            dma((5,)),
            dma((GROUPS - 1,)),
            dma((GROUPS - 1,)),
            dma((MEMBERS - 1,)),
            dma((MEMBERS - 1,)),
            dma((MEMBERS // 2,)),
            dma((MEMBERS,)),
            dma((MEMBERS // 2,)),
            dma((MEMBERS - 1,)),
            dma((MEMBERS - 1,)),
            dma((GROUPS - 1,)),
            dma((GROUPS - 1,)),
        ],
        compiler_params=pltpu.CompilerParams(
            collective_id=0, has_side_effects=True, vmem_limit_bytes=67043328
        ),
    )(
        queries.reshape(QT, DIM),
        candidates.reshape(GROUPS, K),
        storage_row.reshape(16, 128),
        lengths,
        token_cents.reshape(PASSAGES, PT),
        residual_codes.reshape(PASSAGES, PT, DIM),
        centroids,
        bucket_weights,
    )
    return out.reshape(1, 1, GROUPS * K)


def solution(mesh):
    in_specs = (
        P("corpus", "cent", None, None),
        P("corpus", None, "cent", None),
        P("corpus", None),
        P("corpus", "cent"),
        P("corpus", "cent", None),
        P("corpus", "cent", None, None),
        P("cent", None),
        P(),
    )
    out_specs = P("corpus", "cent", None)
    return jax.shard_map(body, mesh=mesh, in_specs=in_specs, out_specs=out_specs, check_vma=False)
```

```python
import jax
import jax.numpy as jnp
from jax import lax
from jax.experimental import pallas as pl
from jax.experimental.pallas import tpu as pltpu
from jax.sharding import PartitionSpec as P

DIM = 128
QT = 32
PT = 128
GROUPS = 8
MEMBERS = 32
K = 32
ENTRIES = 256
CAP = 16
SLOTS = MEMBERS * CAP
PASSAGES = 64
CENTS = 8192
WIDE = 8
CHUNKS = 120
FIRST = 3
BETWEEN = 1
MESH = pl.DeviceIdType.MESH
HIGH = lax.Precision.HIGHEST
NT = (((1,), (1,)), ((), ()))
F32, I32, BF16 = jnp.float32, jnp.int32, jnp.bfloat16


def iota(shape, dim):
    return lax.broadcasted_iota(I32, shape, dim)


def one_hot(flag):
    return jnp.where(flag, F32(1.0), F32(0.0))


def dot(a, b):
    return jnp.dot(a, b, preferred_element_type=F32)


def request_tiles(cand, table, member):
    lanes = iota((32, ENTRIES), 1)
    spread = one_hot(lanes % K == iota((32, ENTRIES), 0))
    wide = jnp.dot(cand.astype(F32), spread, precision=HIGH, preferred_element_type=F32)
    mine = iota((GROUPS, ENTRIES), 1) // K == iota((GROUPS, ENTRIES), 0)
    ident = jnp.sum(jnp.where(mine, wide, 0.0), axis=0, keepdims=True).astype(I32)
    low = one_hot(iota((128, ENTRIES), 0) == (ident & 127))
    looked = jnp.dot(table.astype(F32), low, precision=HIGH, preferred_element_type=F32)
    high = iota((16, ENTRIES), 0) == (ident >> 7)
    row = jnp.sum(jnp.where(high, looked, 0.0), axis=0, keepdims=True).astype(I32)
    owner, stored = row >> 6, row & 63
    owned = one_hot(iota((MEMBERS, ENTRIES), 0) == owner)
    before = one_hot(iota((ENTRIES, ENTRIES), 0) < iota((ENTRIES, ENTRIES), 1))
    ahead = dot(owned.astype(BF16), before.astype(BF16))
    position = jnp.sum(owned * ahead, axis=0, keepdims=True).astype(I32)
    code = (stored * ENTRIES + iota((1, ENTRIES), 1) + 1).astype(F32)
    place = one_hot(iota((128, ENTRIES), 0) == position + (member % 8) * CAP)
    tiles = lax.dot_general(
        owned * code, place, NT, precision=HIGH, preferred_element_type=F32
    )
    return tiles.astype(I32)


def chunk_tables(packed):
    code = jnp.concatenate([packed[r : r + 1, :] for r in range(4)], axis=1)
    there = code > 0
    stored = jnp.where(there, (code - 1) >> 8, PASSAGES)
    entry = jnp.where(there, (code - 1) & 255, 0)
    group, cand = entry >> 5, entry & 31
    source = iota((1, SLOTS), 1) >> 4
    named = one_hot(iota((PASSAGES, SLOTS), 0) == stored)
    before = one_hot(iota((128, 128), 0) < iota((128, 128), 1)).astype(BF16)
    ones = jnp.ones((128, 128), BF16)
    ahead, count = [], jnp.zeros((PASSAGES, 128), F32)
    for r in range(4):
        piece = named[:, 128 * r : 128 * (r + 1)].astype(BF16)
        ahead.append(dot(piece, before) + count)
        count = count + dot(piece, ones)
    ahead = jnp.concatenate(ahead, axis=1)
    position = jnp.sum(named * ahead, axis=0, keepdims=True).astype(I32)
    needed = (count.astype(I32) + (WIDE - 1)) >> 3
    lower = one_hot(iota((PASSAGES, PASSAGES), 1) < iota((PASSAGES, PASSAGES), 0))
    first = dot(lower.astype(BF16), needed.astype(F32).astype(BF16))
    first4 = jnp.concatenate([first] * 4, axis=1)
    chunk = jnp.sum(named * first4, axis=0, keepdims=True).astype(I32) + (position >> 3)
    in_chunk = one_hot((iota((128, SLOTS), 0) == chunk) & there).astype(BF16)
    column = iota((WIDE, SLOTS), 0) == (position & 7)

    def placed(value):
        return jnp.where(column, value.astype(F32), 0.0)

    values = jnp.concatenate(
        [
            placed(source * GROUPS + group),
            placed(source * 2 + (group >> 2) + 1),
            placed((group & 3) * K + cand),
        ],
        axis=0,
    ).astype(BF16)
    tables = lax.dot_general(values, in_chunk, NT, preferred_element_type=F32).astype(I32)
    ends = first.astype(I32) + needed
    passed = jnp.where(ends <= iota((PASSAGES, 128), 1), 1.0, 0.0)
    passage = jnp.sum(passed, axis=0, keepdims=True).astype(I32)
    passage = jnp.minimum(passage, PASSAGES - 1)
    index = jnp.concatenate(
        [tables[0:WIDE], jnp.broadcast_to(passage, (8, 128))], axis=0
    )
    return index, tables[8:16], tables[16:24]


def each(start, stop, step):
    def run(i, carry):
        step(i)
        return carry

    lax.fori_loop(start, stop, run, 0)


def kernel(
    q_hbm,
    cand_hbm,
    table_hbm,
    len_hbm,
    tok_hbm,
    codes_hbm,
    cent_hbm,
    bw_hbm,
    out_ref,
    cand_ref,
    table_ref,
    len_ref,
    tok_ref,
    bw_ref,
    codes,
    cent,
    table32,
    rows_a,
    rows_b,
    embed,
    queries,
    asks,
    asked,
    index_v,
    index_s,
    slot_row,
    slot_lane,
    best,
    part,
    parts,
    last,
    lasts,
    code_sem,
    local_sem,
    z_send,
    z_recv,
    ask_send,
    ask_recv,
    q_send,
    q_recv,
    fwd_send,
    part_send,
    part_recv,
    last_send,
    last_recv,
):
    shard = lax.axis_index("corpus")
    member = lax.axis_index("cent")
    core = member % 2
    chip = member // 2
    partner = chip * 2 + (1 - core)
    chips = MEMBERS // 2

    def peer(step):
        return lax.rem(member + step, MEMBERS)

    def other(step):
        return lax.rem(shard + step, GROUPS)

    def local(src, dst, n):
        return pltpu.make_async_copy(src, dst, local_sem.at[n])

    barrier = pltpu.get_barrier_semaphore()
    each(
        1,
        GROUPS,
        lambda s: pl.semaphore_signal(
            barrier, inc=1, device_id=(other(s), member), device_id_type=MESH
        ),
    )
    each(
        1,
        MEMBERS,
        lambda s: pl.semaphore_signal(
            barrier, inc=1, device_id=(shard, peer(s)), device_id_type=MESH
        ),
    )

    own_query = local(q_hbm, queries.at[member * GROUPS + shard], 0)
    fetches = [
        local(cand_hbm, cand_ref, 1),
        local(table_hbm, table_ref, 2),
        local(len_hbm, len_ref, 3),
        local(tok_hbm, tok_ref, 4),
        local(bw_hbm, bw_ref, 5),
        local(cent_hbm, cent, 6),
    ]
    own_query.start()
    for fetch in fetches:
        fetch.start()

    def code_copy(p):
        return pltpu.make_async_copy(codes_hbm.at[p], codes.at[p], code_sem.at[p])

    each(0, PASSAGES, lambda p: code_copy(p).start())

    def widen(i):
        s = pl.ds(pl.multiple_of(i * 256, 256), 256)
        table32[s, :] = cent[s, :].astype(F32)

    def gather(p, rows, start, size):
        for s in range(start, start + size):
            i = tok_ref[p, s] & (CENTS - 1)
            rows[pl.ds(s, 1), :] = table32[pl.ds(i, 1), :]

    def finish(p, rows, s0, top):
        c = codes[p, pl.ds(s0, 32), :]
        r = jnp.where(c < 2, jnp.where(c == 0, w0, w1), jnp.where(c == 2, w2, w3))
        x = rows[pl.ds(s0, 32), :] + r
        y = x * lax.rsqrt(jnp.sum(x * x, axis=-1, keepdims=True) + 1e-6)
        if s0 == 0:
            top = jnp.broadcast_to(y[0:1, :], (32, DIM))
        y = jnp.where(iota((32, DIM), 0) + s0 < len_ref[0, p], y, top)
        embed[p, pl.ds(s0, 32), :] = y.astype(BF16)
        return top

    def decode(pair):
        p = 2 * pair
        later = jnp.minimum(p + 2, PASSAGES - 1)
        code_copy(p).wait()
        code_copy(p + 1).wait()
        for now, this, nxt, that in ((p, rows_a, p + 1, rows_b), (p + 1, rows_b, later, rows_a)):
            top = None
            for s0 in range(0, PT, 32):
                gather(nxt, that, s0, 32)
                top = finish(now, this, s0, top)

    def z_copy(step):
        return pltpu.make_async_remote_copy(
            src_ref=queries.at[member * GROUPS + shard],
            dst_ref=queries.at[member * GROUPS + shard],
            send_sem=z_send.at[step - 1],
            recv_sem=z_recv.at[step - 1],
            device_id=(other(step), member),
            device_id_type=MESH,
        )

    def q_copy(step, first, size):
        target = lax.rem(chip + step, chips) * 2 + core
        block = pl.ds(member * GROUPS + first, size)
        return pltpu.make_async_remote_copy(
            src_ref=queries.at[block],
            dst_ref=queries.at[block],
            send_sem=q_send.at[step],
            recv_sem=q_recv.at[step],
            device_id=(shard, target),
            device_id_type=MESH,
        )

    def fwd_copy(step):
        source = lax.rem(chip + chips - step, chips) * 2 + core
        block = pl.ds(source * GROUPS, GROUPS)
        return pltpu.make_async_remote_copy(
            src_ref=queries.at[block],
            dst_ref=queries.at[block],
            send_sem=fwd_send.at[step],
            recv_sem=q_recv.at[chips + step],
            device_id=(shard, partner),
            device_id_type=MESH,
        )

    def ask_copy(step):
        return pltpu.make_async_remote_copy(
            src_ref=asks.at[peer(step)],
            dst_ref=asked.at[member],
            send_sem=ask_send.at[step - 1],
            recv_sem=ask_recv.at[step - 1],
            device_id=(shard, peer(step)),
            device_id_type=MESH,
        )

    own_query.wait()
    pl.semaphore_wait(barrier, MEMBERS + GROUPS - 2)
    each(1, GROUPS, lambda s: z_copy(s).start())
    each(1, chips, lambda s: q_copy(s, shard, 1).start())
    for fetch in fetches[:2]:
        fetch.wait()
    tiles = request_tiles(cand_ref[...], table_ref[...], member)
    row = iota((8, 128), 0) == member // 8
    for m in range(MEMBERS):
        asks[m] = jnp.where(row, jnp.broadcast_to(tiles[m : m + 1, :], (8, 128)), 0)
    each(1, MEMBERS, lambda s: ask_copy(s).start())
    for fetch in fetches[2:]:
        fetch.wait()
    each(0, CENTS // 256, widen)
    w0, w1, w2, w3 = bw_ref[0], bw_ref[1], bw_ref[2], bw_ref[3]

    def pass_on(k):
        at = FIRST + k * BETWEEN
        each(at, at + BETWEEN, decode)
        far = k // 2 + 1
        step = far + (k % 2) * (GROUPS - 2 * far)
        z_copy(step).wait_recv()
        source = lax.rem(shard + GROUPS - step, GROUPS)
        each(1, chips, lambda s: q_copy(s, source, 1).start())

    gather(0, rows_a, 0, PT)
    each(0, FIRST, decode)
    each(0, GROUPS - 1, pass_on)
    fwd_copy(0).start()
    each(FIRST + (GROUPS - 1) * BETWEEN, PASSAGES // 2, decode)

    asked[member] = asks[member]
    each(1, MEMBERS, lambda s: ask_copy(s).wait())
    packed = asked[0]
    for m in range(1, MEMBERS):
        packed = packed + asked[m]
    index, srow, slane = chunk_tables(packed)
    index_v[...] = index
    slot_row[...] = srow
    slot_lane[...] = slane
    index_copy = local(index_v, index_s, 0)
    index_copy.start()

    def relay(step):
        q_copy(step, 0, GROUPS).wait()
        fwd_copy(step).start()

    each(1, chips, relay)
    index_copy.wait()
    each(1, GROUPS, lambda s: z_copy(s).wait_send())
    each(0, chips, lambda s: fwd_copy(s).wait())

    best[pl.ds(CHUNKS, 128 - CHUNKS), :] = jnp.zeros((128 - CHUNKS, WIDE * QT), F32)

    def score(b):
        found = []
        for u in range(8):
            ch = b * 8 + u
            e = embed[index_s[8, ch] & (PASSAGES - 1)]
            q = jnp.concatenate(
                [queries[index_s[j, ch] & 255] for j in range(WIDE)], axis=0
            )
            dots = lax.dot_general(e, q, NT, preferred_element_type=F32)
            found.append(jnp.max(dots, axis=0, keepdims=True))
        best[pl.ds(pl.multiple_of(b * 8, 8), 8), :] = jnp.concatenate(found, axis=0)

    each(0, CHUNKS // 8, score)

    gather = one_hot(iota((WIDE, WIDE * QT), 1) // QT == iota((WIDE, WIDE * QT), 0))
    total = lax.dot_general(
        gather, best[...], NT, precision=HIGH, preferred_element_type=F32
    )
    left, right = [], []
    for j in range(WIDE):
        at = iota((64, 128), 0) + 1 == slot_row[j : j + 1, :]
        left.append(jnp.where(at, jnp.broadcast_to(total[j : j + 1, :], (64, 128)), 0.0))
        right.append(one_hot(iota((128, 128), 0) == slot_lane[j : j + 1, :]))
    table = lax.dot_general(
        jnp.concatenate(left, axis=1),
        jnp.concatenate(right, axis=1),
        NT,
        precision=HIGH,
        preferred_element_type=F32,
    )
    for m in range(MEMBERS):
        part[m] = table[2 * m : 2 * m + 2, :]

    def part_copy(step):
        return pltpu.make_async_remote_copy(
            src_ref=part.at[peer(step)],
            dst_ref=parts.at[member],
            send_sem=part_send.at[step - 1],
            recv_sem=part_recv.at[step - 1],
            device_id=(shard, peer(step)),
            device_id_type=MESH,
        )

    each(1, MEMBERS, lambda s: part_copy(s).start())
    parts[member] = part[member]
    each(1, MEMBERS, lambda s: part_copy(s).wait())
    tot = parts[0]
    for m in range(1, MEMBERS):
        tot = tot + parts[m]

    quarter = iota((8, 128), 1) // K == shard % 4
    row_in = iota((2, 128), 0) == shard // 4
    for o in range(GROUPS):
        line = jnp.broadcast_to(tot[o // 4 : o // 4 + 1, :], (8, 128))
        shift = lax.rem(shard + 4 - o % 4, 4) * K
        line = jnp.where(quarter, pltpu.roll(line, shift, 1), 0.0)
        last[o] = jnp.where(row_in, line[0:2, :], 0.0)

    def last_copy(step):
        return pltpu.make_async_remote_copy(
            src_ref=last.at[other(step)],
            dst_ref=lasts.at[shard],
            send_sem=last_send.at[step - 1],
            recv_sem=last_recv.at[step - 1],
            device_id=(other(step), member),
            device_id_type=MESH,
        )

    each(1, GROUPS, lambda s: last_copy(s).start())
    lasts[shard] = last[shard]
    each(1, GROUPS, lambda s: last_copy(s).wait())
    scores = lasts[0]
    for o in range(1, GROUPS):
        scores = scores + lasts[o]
    out_ref[...] = scores


def body(
    queries,
    candidates,
    storage_row,
    lengths,
    token_cents,
    residual_codes,
    centroids,
    bucket_weights,
):
    vmem = pl.BlockSpec(memory_space=pltpu.VMEM)
    hbm = pl.BlockSpec(memory_space=pl.ANY)
    dma = pltpu.SemaphoreType.DMA
    out = pl.pallas_call(
        kernel,
        out_shape=jax.ShapeDtypeStruct((2, 128), F32),
        in_specs=[hbm] * 8,
        out_specs=vmem,
        scratch_shapes=[
            pltpu.VMEM((GROUPS, K), I32),
            pltpu.VMEM((16, 128), I32),
            pltpu.SMEM((1, PASSAGES), I32),
            pltpu.SMEM((PASSAGES, PT), I32),
            pltpu.SMEM((4,), F32),
            pltpu.VMEM((PASSAGES, PT, DIM), I32),
            pltpu.VMEM((CENTS, DIM), BF16),
            pltpu.VMEM((CENTS, DIM), F32),
            pltpu.VMEM((PT, DIM), F32),
            pltpu.VMEM((PT, DIM), F32),
            pltpu.VMEM((PASSAGES, PT, DIM), BF16),
            pltpu.VMEM((MEMBERS * GROUPS, QT, DIM), BF16),
            pltpu.VMEM((MEMBERS, 8, 128), I32),
            pltpu.VMEM((MEMBERS, 8, 128), I32),
            pltpu.VMEM((16, 128), I32),
            pltpu.SMEM((16, 128), I32),
            pltpu.VMEM((8, 128), I32),
            pltpu.VMEM((8, 128), I32),
            pltpu.VMEM((128, WIDE * QT), F32),
            pltpu.VMEM((MEMBERS, 2, 128), F32),
            pltpu.VMEM((MEMBERS, 2, 128), F32),
            pltpu.VMEM((GROUPS, 2, 128), F32),
            pltpu.VMEM((GROUPS, 2, 128), F32),
            dma((PASSAGES,)),
            dma((7,)),
            dma((GROUPS - 1,)),
            dma((GROUPS - 1,)),
            dma((MEMBERS - 1,)),
            dma((MEMBERS - 1,)),
            dma((MEMBERS // 2,)),
            dma((MEMBERS,)),
            dma((MEMBERS // 2,)),
            dma((MEMBERS - 1,)),
            dma((MEMBERS - 1,)),
            dma((GROUPS - 1,)),
            dma((GROUPS - 1,)),
        ],
        compiler_params=pltpu.CompilerParams(
            collective_id=0, has_side_effects=True, vmem_limit_bytes=67043328
        ),
    )(
        queries.reshape(QT, DIM),
        candidates.reshape(GROUPS, K),
        storage_row.reshape(16, 128),
        lengths,
        token_cents.reshape(PASSAGES, PT),
        residual_codes.reshape(PASSAGES, PT, DIM),
        centroids,
        bucket_weights,
    )
    return out.reshape(1, 1, GROUPS * K)


def solution(mesh):
    in_specs = (
        P("corpus", "cent", None, None),
        P("corpus", None, "cent", None),
        P("corpus", None),
        P("corpus", "cent"),
        P("corpus", "cent", None),
        P("corpus", "cent", None, None),
        P("cent", None),
        P(),
    )
    out_specs = P("corpus", "cent", None)
    return jax.shard_map(body, mesh=mesh, in_specs=in_specs, out_specs=out_specs, check_vma=False)
```

```python
import jax
import jax.numpy as jnp
from jax import lax
from jax.experimental import pallas as pl
from jax.experimental.pallas import tpu as pltpu
from jax.sharding import PartitionSpec as P

DIM = 128
QT = 32
PT = 128
GROUPS = 8
MEMBERS = 32
K = 32
ENTRIES = 256
CAP = 16
SLOTS = MEMBERS * CAP
PASSAGES = 64
CENTS = 8192
WIDE = 8
DEEP = 3
CHUNKS = 120
FIRST = 8
SECOND = 2
THIRD = 6
FOURTH = 3
MESH = pl.DeviceIdType.MESH
HIGH = lax.Precision.HIGHEST
NT = (((1,), (1,)), ((), ()))
F32, I32, BF16 = jnp.float32, jnp.int32, jnp.bfloat16


def iota(shape, dim):
    return lax.broadcasted_iota(I32, shape, dim)


def one_hot(flag):
    return jnp.where(flag, F32(1.0), F32(0.0))


def dot(a, b):
    return jnp.dot(a, b, preferred_element_type=F32)


def request_tiles(cand, table, member):
    lanes = iota((32, ENTRIES), 1)
    spread = one_hot(lanes % K == iota((32, ENTRIES), 0))
    wide = jnp.dot(cand.astype(F32), spread, precision=HIGH, preferred_element_type=F32)
    mine = iota((GROUPS, ENTRIES), 1) // K == iota((GROUPS, ENTRIES), 0)
    ident = jnp.sum(jnp.where(mine, wide, 0.0), axis=0, keepdims=True).astype(I32)
    low = one_hot(iota((128, ENTRIES), 0) == (ident & 127))
    looked = jnp.dot(table.astype(F32), low, precision=HIGH, preferred_element_type=F32)
    high = iota((16, ENTRIES), 0) == (ident >> 7)
    row = jnp.sum(jnp.where(high, looked, 0.0), axis=0, keepdims=True).astype(I32)
    owner, stored = row >> 6, row & 63
    owned = one_hot(iota((MEMBERS, ENTRIES), 0) == owner)
    before = one_hot(iota((ENTRIES, ENTRIES), 0) < iota((ENTRIES, ENTRIES), 1))
    ahead = dot(owned.astype(BF16), before.astype(BF16))
    position = jnp.sum(owned * ahead, axis=0, keepdims=True).astype(I32)
    code = (stored * ENTRIES + iota((1, ENTRIES), 1) + 1).astype(F32)
    place = one_hot(iota((128, ENTRIES), 0) == position + (member % 8) * CAP)
    tiles = lax.dot_general(
        owned * code, place, NT, precision=HIGH, preferred_element_type=F32
    )
    return tiles.astype(I32)


def order(step):
    return jnp.where(step == 0, 0, jnp.where(step > 4, 2 * (GROUPS - step), 2 * step - 1))


def chunk_tables(packed, shard):
    code = jnp.concatenate([packed[r : r + 1, :] for r in range(4)], axis=1)
    there = code > 0
    stored = jnp.where(there, (code - 1) >> 8, PASSAGES)
    entry = jnp.where(there, (code - 1) & 255, 0)
    group, cand = entry >> 5, entry & 31
    source = iota((1, SLOTS), 1) >> 4
    kept = (source & 1) * 128 + (source >> 1) * GROUPS + order((shard + GROUPS - group) & 7)
    named = one_hot(iota((PASSAGES, SLOTS), 0) == stored)
    before = one_hot(iota((128, 128), 0) < iota((128, 128), 1)).astype(BF16)
    ones = jnp.ones((128, 128), BF16)
    ahead, count = [], jnp.zeros((PASSAGES, 128), F32)
    for r in range(4):
        piece = named[:, 128 * r : 128 * (r + 1)].astype(BF16)
        ahead.append(dot(piece, before) + count)
        count = count + dot(piece, ones)
    ahead = jnp.concatenate(ahead, axis=1)
    position = jnp.sum(named * ahead, axis=0, keepdims=True).astype(I32)
    needed = (count.astype(I32) + (WIDE - 1)) >> 3
    lower = one_hot(iota((PASSAGES, PASSAGES), 1) < iota((PASSAGES, PASSAGES), 0))
    first = dot(lower.astype(BF16), needed.astype(F32).astype(BF16))
    first4 = jnp.concatenate([first] * 4, axis=1)
    chunk = jnp.sum(named * first4, axis=0, keepdims=True).astype(I32) + (position >> 3)
    in_chunk = one_hot((iota((128, SLOTS), 0) == chunk) & there).astype(BF16)
    column = iota((WIDE, SLOTS), 0) == (position & 7)

    def placed(value):
        return jnp.where(column, value.astype(F32), 0.0)

    values = jnp.concatenate(
        [
            placed(kept),
            placed(source * 2 + (group >> 2) + 1),
            placed((group & 3) * K + cand),
        ],
        axis=0,
    ).astype(BF16)
    tables = lax.dot_general(values, in_chunk, NT, preferred_element_type=F32).astype(I32)
    ends = first.astype(I32) + needed
    passed = jnp.where(ends <= iota((PASSAGES, 128), 1), 1.0, 0.0)
    passage = jnp.sum(passed, axis=0, keepdims=True).astype(I32)
    passage = jnp.minimum(passage, PASSAGES - 1)
    index = jnp.concatenate(
        [tables[0:WIDE], jnp.broadcast_to(passage, (8, 128))], axis=0
    )
    return index, tables[8:16], tables[16:24]


def each(start, stop, step):
    def run(i, carry):
        step(i)
        return carry

    lax.fori_loop(start, stop, run, 0)


def kernel(
    q_hbm,
    cand_hbm,
    table_hbm,
    len_hbm,
    tok_hbm,
    codes_hbm,
    cent_hbm,
    bw_hbm,
    out_ref,
    cand_ref,
    table_ref,
    len_ref,
    tok_v,
    tok_ref,
    bw_ref,
    codes,
    cent,
    table32,
    rows_a,
    rows_b,
    embed,
    queries,
    asks,
    asked,
    index_v,
    index_s,
    rows_of,
    lanes_of,
    best,
    part,
    parts,
    last,
    lasts,
    code_sem,
    local_sem,
    z_send,
    z_recv,
    ask_send,
    ask_recv,
    near_send,
    near_recv,
    relay_send,
    far_recv,
    fwd_send,
    fwd_recv,
    part_send,
    part_recv,
    last_send,
    last_recv,
):
    shard = lax.axis_index("corpus")
    member = lax.axis_index("cent")
    core = member % 2
    chip = member // 2
    partner = chip * 2 + (1 - core)
    chip_x, chip_y = chip // 4, chip % 4
    mine = core * 128 + chip * GROUPS

    def peer(step):
        return lax.rem(member + step, MEMBERS)

    def other(step):
        return lax.rem(shard + step, GROUPS)

    def local(src, dst, n):
        return pltpu.make_async_copy(src, dst, local_sem.at[n])

    barrier = pltpu.get_barrier_semaphore()
    each(
        1,
        GROUPS,
        lambda s: pl.semaphore_signal(
            barrier, inc=1, device_id=(other(s), member), device_id_type=MESH
        ),
    )
    each(
        1,
        MEMBERS,
        lambda s: pl.semaphore_signal(
            barrier, inc=1, device_id=(shard, peer(s)), device_id_type=MESH
        ),
    )

    own_query = local(q_hbm, queries.at[mine], 0)
    fetches = [
        local(cand_hbm, cand_ref, 1),
        local(table_hbm, table_ref, 2),
        local(len_hbm, len_ref, 3),
        local(tok_hbm, tok_v, 4),
        local(bw_hbm, bw_ref, 5),
        local(cent_hbm, cent, 6),
    ]
    own_query.start()
    for fetch in fetches:
        fetch.start()

    def code_copy(p):
        return pltpu.make_async_copy(codes_hbm.at[p], codes.at[p], code_sem.at[p])

    each(0, PASSAGES, lambda p: code_copy(p).start())

    def widen(i):
        s = pl.ds(pl.multiple_of(i * 256, 256), 256)
        table32[s, :] = cent[s, :].astype(F32)

    def gather(p, rows, start, size):
        ids = tok_ref.at[p]
        for s in range(start, start + size):
            rows[pl.ds(s, 1), :] = table32[pl.ds(ids[s], 1), :]

    def finish(p, rows, s0, top):
        w0, w1, w2, w3 = bw_ref[0], bw_ref[1], bw_ref[2], bw_ref[3]
        c = codes[p, pl.ds(s0, 32), :]
        r = jnp.where(c < 2, jnp.where(c == 0, w0, w1), jnp.where(c == 2, w2, w3))
        x = rows[pl.ds(s0, 32), :] + r
        y = x * lax.rsqrt(jnp.sum(x * x, axis=-1, keepdims=True) + 1e-6)
        if s0 == 0:
            top = jnp.broadcast_to(y[0:1, :], (32, DIM))
        y = jnp.where(iota((32, DIM), 0) + s0 < len_ref[0, p], y, top)
        embed[p, pl.ds(s0, 32), :] = y.astype(BF16)
        return top

    def decode(pair):
        p = 2 * pair
        later = jnp.minimum(p + 2, PASSAGES - 1)
        code_copy(p).wait()
        code_copy(p + 1).wait()
        for now, this, nxt, that in ((p, rows_a, p + 1, rows_b), (p + 1, rows_b, later, rows_a)):
            top = None
            for s0 in range(0, PT, 32):
                gather(nxt, that, s0, 32)
                top = finish(now, this, s0, top)

    def z_copy(step):
        return pltpu.make_async_remote_copy(
            src_ref=queries.at[mine],
            dst_ref=queries.at[mine + order(step)],
            send_sem=z_send.at[step - 1],
            recv_sem=z_recv.at[step - 1],
            device_id=(other(step), member),
            device_id_type=MESH,
        )

    def moved(axis, d):
        return lax.rem(chip_x + d * (1 - axis), 4) * 4 + lax.rem(chip_y + d * axis, 4)

    def near_copy(axis, d, half):
        block = queries.at[pl.ds(mine + 4 * half, 4)]
        return pltpu.make_async_remote_copy(
            src_ref=block,
            dst_ref=block,
            send_sem=near_send.at[axis, d, half],
            recv_sem=near_recv.at[axis, d, half],
            device_id=(shard, moved(axis, d) * 2 + core),
            device_id_type=MESH,
        )

    def relay_copy(half, d, e):
        source = moved(half, 4 - d)
        block = queries.at[pl.ds(core * 128 + source * GROUPS + 4 * half, 4)]
        return pltpu.make_async_remote_copy(
            src_ref=block,
            dst_ref=block,
            send_sem=relay_send.at[half, d, e],
            recv_sem=far_recv.at[d * (1 - half) + e * half, d * half + e * (1 - half)],
            device_id=(shard, moved(1 - half, e) * 2 + core),
            device_id_type=MESH,
        )

    def source_block(dx, dy):
        source = lax.rem(chip_x + 4 - dx, 4) * 4 + lax.rem(chip_y + 4 - dy, 4)
        return queries.at[pl.ds(core * 128 + source * GROUPS, GROUPS)]

    def exchanged(src, dst, send, recv, count):
        pltpu.make_async_remote_copy(
            src_ref=src.at[pl.ds(0, count)],
            dst_ref=dst.at[pl.ds(0, count)],
            send_sem=send,
            recv_sem=recv,
            device_id=(shard, partner),
            device_id_type=MESH,
        ).wait()

    def fwd_copy(dx, dy):
        block = source_block(dx, dy)
        return pltpu.make_async_remote_copy(
            src_ref=block,
            dst_ref=block,
            send_sem=fwd_send.at[dx, dy],
            recv_sem=fwd_recv.at[dx, dy],
            device_id=(shard, partner),
            device_id_type=MESH,
        )

    def far_wait(dx, dy):
        block = source_block(dx, dy)
        pltpu.make_async_remote_copy(
            src_ref=block,
            dst_ref=block,
            send_sem=fwd_send.at[dx, dy],
            recv_sem=far_recv.at[dx, dy],
            device_id=(shard, partner),
            device_id_type=MESH,
        ).wait_recv()

    def ask_copy(step):
        return pltpu.make_async_remote_copy(
            src_ref=asks.at[peer(step)],
            dst_ref=asked.at[member],
            send_sem=ask_send,
            recv_sem=ask_recv,
            device_id=(shard, peer(step)),
            device_id_type=MESH,
        )

    def send_near(half):
        for axis in range(2):
            each(1, 4, lambda d: near_copy(axis, d, half).start())

    def relay(half):
        def one(d):
            near_copy(half, d, half).wait_recv()
            each(1, 4, lambda e: relay_copy(half, d, e).start())

        each(1, 4, one)

    own_query.wait()
    pl.semaphore_wait(barrier, MEMBERS + GROUPS - 2)
    each(1, GROUPS, lambda s: z_copy(s).start())
    for fetch in fetches[:2]:
        fetch.wait()
    tiles = request_tiles(cand_ref[...], table_ref[...], member)
    row = iota((8, 128), 0) == member // 8
    for m in range(MEMBERS):
        asks[m] = jnp.where(row, jnp.broadcast_to(tiles[m : m + 1, :], (8, 128)), 0)
    each(1, MEMBERS, lambda s: ask_copy(s).start())
    fetches[3].wait()
    tok_v[...] = tok_v[...] & (CENTS - 1)
    ids_copy = local(tok_v, tok_ref, 4)
    ids_copy.start()
    for fetch in fetches[2:3] + fetches[4:]:
        fetch.wait()
    each(0, CENTS // 256, widen)
    ids_copy.wait()
    gather(0, rows_a, 0, PT)

    each(0, FIRST, decode)
    for step in (1, 7, 2):
        z_copy(step).wait_recv()
    send_near(0)
    done = FIRST + SECOND
    each(FIRST, done, decode)
    for step in (6, 3, 5, 4):
        z_copy(step).wait_recv()
    send_near(1)
    fwd_copy(0, 0).start()
    each(done, done + THIRD, decode)
    done = done + THIRD
    relay(0)
    each(done, done + FOURTH, decode)
    done = done + FOURTH
    relay(1)
    each(done, PASSAGES // 2, decode)

    asked[member] = asks[member]
    exchanged(asks, asked, ask_send, ask_recv, MEMBERS - 1)
    packed = asked[0]
    for m in range(1, MEMBERS):
        packed = packed + asked[m]
    index, srow, slane = chunk_tables(packed, shard)
    index_v[...] = index
    index_copy = local(index_v, index_s, 0)
    index_copy.start()
    for j in range(WIDE):
        lane = slice(128 * j, 128 * (j + 1))
        rows_of[:, lane] = one_hot(iota((64, 128), 0) + 1 == srow[j : j + 1, :]).astype(BF16)
        lanes_of[:, lane] = one_hot(iota((128, 128), 0) == slane[j : j + 1, :]).astype(BF16)

    each(1, 4, lambda d: near_copy(1, d, 0).wait_recv())
    each(1, 4, lambda d: near_copy(0, d, 1).wait_recv())
    each(1, 4, lambda d: fwd_copy(d, 0).start())
    each(1, 4, lambda d: fwd_copy(0, d).start())

    def far_on(n):
        dx, dy = n // 3 + 1, n % 3 + 1
        far_wait(dx, dy)
        fwd_copy(dx, dy).start()

    each(0, 9, far_on)
    index_copy.wait()
    each(1, GROUPS, lambda s: z_copy(s).wait_send())

    def near_sent(n):
        for axis in range(2):
            near_copy(axis, n // 2 + 1, n % 2).wait_send()

    def relays_sent(n):
        for half in range(2):
            relay_copy(half, n // 3 + 1, n % 3 + 1).wait_send()

    each(0, 16, lambda n: fwd_copy(n // 4, n % 4).wait())

    best[pl.ds(CHUNKS, 128 - CHUNKS), :] = jnp.zeros((128 - CHUNKS, WIDE * QT), F32)

    def score(b):
        for v in range(DEEP):
            found = []
            for u in range(8):
                ch = (b * DEEP + v) * 8 + u
                e = embed[index_s[8, ch] & (PASSAGES - 1)]
                q = jnp.concatenate(
                    [queries[index_s[j, ch] & 255] for j in range(WIDE)], axis=0
                )
                dots = lax.dot_general(e, q, NT, preferred_element_type=F32)
                found.append(jnp.max(dots, axis=0, keepdims=True))
            start = pl.multiple_of((b * DEEP + v) * 8, 8)
            best[pl.ds(start, 8), :] = jnp.concatenate(found, axis=0)

    each(0, CHUNKS // 8 // DEEP, score)

    gather32 = one_hot(iota((WIDE, WIDE * QT), 1) // QT == iota((WIDE, WIDE * QT), 0))
    gather32 = gather32.astype(BF16)

    def thirds(x):
        a = x.astype(BF16)
        b = (x - a.astype(F32)).astype(BF16)
        c = (x - a.astype(F32) - b.astype(F32)).astype(BF16)
        return a, b, c

    total = jnp.zeros((WIDE, 128), F32)
    for piece in thirds(best[...]):
        total = total + lax.dot_general(gather32, piece, NT, preferred_element_type=F32)
    left = []
    for piece in thirds(total):
        left.append(
            jnp.concatenate(
                [
                    rows_of[:, 128 * j : 128 * (j + 1)]
                    * jnp.broadcast_to(piece[j : j + 1, :], (64, 128))
                    for j in range(WIDE)
                ],
                axis=1,
            )
        )
    table = lax.dot_general(
        jnp.concatenate(left, axis=0), lanes_of[...], NT, preferred_element_type=F32
    )
    table = table[0:64] + table[64:128] + table[128:192]
    for m in range(MEMBERS):
        part[m] = table[2 * m : 2 * m + 2, :]

    def part_copy(step):
        return pltpu.make_async_remote_copy(
            src_ref=part.at[peer(step)],
            dst_ref=parts.at[member],
            send_sem=part_send,
            recv_sem=part_recv,
            device_id=(shard, peer(step)),
            device_id_type=MESH,
        )

    each(1, MEMBERS, lambda s: part_copy(s).start())
    parts[member] = part[member]
    each(0, 6, near_sent)
    each(0, 9, relays_sent)
    exchanged(part, parts, part_send, part_recv, MEMBERS - 1)
    tot = parts[0]
    for m in range(1, MEMBERS):
        tot = tot + parts[m]

    quarter = iota((8, 128), 1) // K == shard % 4
    row_in = iota((2, 128), 0) == shard // 4
    for o in range(GROUPS):
        line = jnp.broadcast_to(tot[o // 4 : o // 4 + 1, :], (8, 128))
        shift = lax.rem(shard + 4 - o % 4, 4) * K
        line = jnp.where(quarter, pltpu.roll(line, shift, 1), 0.0)
        last[o] = jnp.where(row_in, line[0:2, :], 0.0)

    def last_copy(step):
        return pltpu.make_async_remote_copy(
            src_ref=last.at[other(step)],
            dst_ref=lasts.at[shard],
            send_sem=last_send,
            recv_sem=last_recv,
            device_id=(other(step), member),
            device_id_type=MESH,
        )

    each(1, GROUPS, lambda s: last_copy(s).start())
    lasts[shard] = last[shard]
    exchanged(last, lasts, last_send, last_recv, GROUPS - 1)
    scores = lasts[0]
    for o in range(1, GROUPS):
        scores = scores + lasts[o]
    out_ref[...] = scores


def body(
    queries,
    candidates,
    storage_row,
    lengths,
    token_cents,
    residual_codes,
    centroids,
    bucket_weights,
):
    vmem = pl.BlockSpec(memory_space=pltpu.VMEM)
    hbm = pl.BlockSpec(memory_space=pl.ANY)
    dma = pltpu.SemaphoreType.DMA
    out = pl.pallas_call(
        kernel,
        out_shape=jax.ShapeDtypeStruct((2, 128), F32),
        in_specs=[hbm] * 8,
        out_specs=vmem,
        scratch_shapes=[
            pltpu.VMEM((GROUPS, K), I32),
            pltpu.VMEM((16, 128), I32),
            pltpu.SMEM((1, PASSAGES), I32),
            pltpu.VMEM((PASSAGES, PT), I32),
            pltpu.SMEM((PASSAGES, PT), I32),
            pltpu.SMEM((4,), F32),
            pltpu.VMEM((PASSAGES, PT, DIM), I32),
            pltpu.VMEM((CENTS, DIM), BF16),
            pltpu.VMEM((CENTS, DIM), F32),
            pltpu.VMEM((PT, DIM), F32),
            pltpu.VMEM((PT, DIM), F32),
            pltpu.VMEM((PASSAGES, PT, DIM), BF16),
            pltpu.VMEM((MEMBERS * GROUPS, QT, DIM), BF16),
            pltpu.VMEM((MEMBERS, 8, 128), I32),
            pltpu.VMEM((MEMBERS, 8, 128), I32),
            pltpu.VMEM((16, 128), I32),
            pltpu.SMEM((16, 128), I32),
            pltpu.VMEM((64, WIDE * 128), BF16),
            pltpu.VMEM((128, WIDE * 128), BF16),
            pltpu.VMEM((128, WIDE * QT), F32),
            pltpu.VMEM((MEMBERS, 2, 128), F32),
            pltpu.VMEM((MEMBERS, 2, 128), F32),
            pltpu.VMEM((GROUPS, 2, 128), F32),
            pltpu.VMEM((GROUPS, 2, 128), F32),
            dma((PASSAGES,)),
            dma((7,)),
            dma((GROUPS - 1,)),
            dma((GROUPS - 1,)),
            dma,
            dma,
            dma((2, 4, 2)),
            dma((2, 4, 2)),
            dma((2, 4, 4)),
            dma((4, 4)),
            dma((4, 4)),
            dma((4, 4)),
            dma,
            dma,
            dma,
            dma,
        ],
        compiler_params=pltpu.CompilerParams(
            collective_id=0, has_side_effects=True, vmem_limit_bytes=67043328
        ),
    )(
        queries.reshape(QT, DIM),
        candidates.reshape(GROUPS, K),
        storage_row.reshape(16, 128),
        lengths,
        token_cents.reshape(PASSAGES, PT),
        residual_codes.reshape(PASSAGES, PT, DIM),
        centroids,
        bucket_weights,
    )
    return out.reshape(1, 1, GROUPS * K)


def solution(mesh):
    in_specs = (
        P("corpus", "cent", None, None),
        P("corpus", None, "cent", None),
        P("corpus", None),
        P("corpus", "cent"),
        P("corpus", "cent", None),
        P("corpus", "cent", None, None),
        P("cent", None),
        P(),
    )
    out_specs = P("corpus", "cent", None)
    return jax.shard_map(body, mesh=mesh, in_specs=in_specs, out_specs=out_specs, check_vma=False)
```

```python
import jax
import jax.numpy as jnp
from jax import lax
from jax.experimental import pallas as pl
from jax.experimental.pallas import tpu as pltpu
from jax.sharding import PartitionSpec as P

DIM = 128
QT = 32
PT = 128
GROUPS = 8
MEMBERS = 32
K = 32
ENTRIES = 256
CAP = 16
SLOTS = MEMBERS * CAP
PASSAGES = 64
CENTS = 8192
WIDE = 8
DEEP = 5
CHUNKS = 120
FIRST = 8
SECOND = 2
THIRD = 6
FOURTH = 3
MESH = pl.DeviceIdType.MESH


def ring(d, n):
    return min(d, n - d)


FARTHEST_MEMBERS = sorted(
    range(1, MEMBERS), key=lambda s: -ring(s // 8, 4) - ring(s // 2 % 4, 4)
)
FARTHEST_SHARDS = sorted(range(1, GROUPS), key=lambda s: -ring(s, GROUPS))
HIGH = lax.Precision.HIGHEST
NT = (((1,), (1,)), ((), ()))
F32, I32, BF16 = jnp.float32, jnp.int32, jnp.bfloat16


def iota(shape, dim):
    return lax.broadcasted_iota(I32, shape, dim)


def one_hot(flag):
    return jnp.where(flag, F32(1.0), F32(0.0))


def dot(a, b):
    return jnp.dot(a, b, preferred_element_type=F32)


def request_tiles(cand, table, member):
    lanes = iota((32, ENTRIES), 1)
    spread = one_hot(lanes % K == iota((32, ENTRIES), 0))
    wide = jnp.dot(cand.astype(F32), spread, precision=HIGH, preferred_element_type=F32)
    mine = iota((GROUPS, ENTRIES), 1) // K == iota((GROUPS, ENTRIES), 0)
    ident = jnp.sum(jnp.where(mine, wide, 0.0), axis=0, keepdims=True).astype(I32)
    low = one_hot(iota((128, ENTRIES), 0) == (ident & 127))
    looked = jnp.dot(table.astype(F32), low, precision=HIGH, preferred_element_type=F32)
    high = iota((16, ENTRIES), 0) == (ident >> 7)
    row = jnp.sum(jnp.where(high, looked, 0.0), axis=0, keepdims=True).astype(I32)
    owner, stored = row >> 6, row & 63
    owned = one_hot(iota((MEMBERS, ENTRIES), 0) == owner)
    before = one_hot(iota((ENTRIES, ENTRIES), 0) < iota((ENTRIES, ENTRIES), 1))
    ahead = dot(owned.astype(BF16), before.astype(BF16))
    position = jnp.sum(owned * ahead, axis=0, keepdims=True).astype(I32)
    code = (stored * ENTRIES + iota((1, ENTRIES), 1) + 1).astype(F32)
    place = one_hot(iota((128, ENTRIES), 0) == position + (member % 8) * CAP)
    tiles = lax.dot_general(
        owned * code, place, NT, precision=HIGH, preferred_element_type=F32
    )
    return tiles.astype(I32)


def order(step):
    return jnp.where(step == 0, 0, jnp.where(step > 4, 2 * (GROUPS - step), 2 * step - 1))


def chunk_tables(packed, shard):
    code = jnp.concatenate([packed[r : r + 1, :] for r in range(4)], axis=1)
    there = code > 0
    stored = jnp.where(there, (code - 1) >> 8, PASSAGES)
    entry = jnp.where(there, (code - 1) & 255, 0)
    group, cand = entry >> 5, entry & 31
    source = iota((1, SLOTS), 1) >> 4
    kept = (source & 1) * 128 + (source >> 1) * GROUPS + order((shard + GROUPS - group) & 7)
    named = one_hot(iota((PASSAGES, SLOTS), 0) == stored)
    before = one_hot(iota((128, 128), 0) < iota((128, 128), 1)).astype(BF16)
    ones = jnp.ones((128, 128), BF16)
    ahead, count = [], jnp.zeros((PASSAGES, 128), F32)
    for r in range(4):
        piece = named[:, 128 * r : 128 * (r + 1)].astype(BF16)
        ahead.append(dot(piece, before) + count)
        count = count + dot(piece, ones)
    ahead = jnp.concatenate(ahead, axis=1)
    position = jnp.sum(named * ahead, axis=0, keepdims=True).astype(I32)
    needed = (count.astype(I32) + (WIDE - 1)) >> 3
    lower = one_hot(iota((PASSAGES, PASSAGES), 1) < iota((PASSAGES, PASSAGES), 0))
    first = dot(lower.astype(BF16), needed.astype(F32).astype(BF16))
    first4 = jnp.concatenate([first] * 4, axis=1)
    chunk = jnp.sum(named * first4, axis=0, keepdims=True).astype(I32) + (position >> 3)
    in_chunk = one_hot((iota((128, SLOTS), 0) == chunk) & there).astype(BF16)
    column = iota((WIDE, SLOTS), 0) == (position & 7)

    def placed(value):
        return jnp.where(column, value.astype(F32), 0.0)

    values = jnp.concatenate(
        [
            placed(kept),
            placed(source * 2 + (group >> 2) + 1),
            placed((group & 3) * K + cand),
        ],
        axis=0,
    ).astype(BF16)
    tables = lax.dot_general(values, in_chunk, NT, preferred_element_type=F32).astype(I32)
    ends = first.astype(I32) + needed
    passed = jnp.where(ends <= iota((PASSAGES, 128), 1), 1.0, 0.0)
    passage = jnp.sum(passed, axis=0, keepdims=True).astype(I32)
    passage = jnp.minimum(passage, PASSAGES - 1)
    index = jnp.concatenate(
        [tables[0:WIDE], jnp.broadcast_to(passage, (8, 128))], axis=0
    )
    return index, tables[8:16], tables[16:24]


def each(start, stop, step):
    def run(i, carry):
        step(i)
        return carry

    lax.fori_loop(start, stop, run, 0)


def kernel(
    q_hbm,
    cand_hbm,
    table_hbm,
    len_hbm,
    tok_hbm,
    codes_hbm,
    cent_hbm,
    bw_hbm,
    lasts,
    cand_ref,
    table_ref,
    len_ref,
    tok_v,
    tok_ref,
    bw_ref,
    codes,
    cent,
    table32,
    rows_a,
    rows_b,
    embed,
    queries,
    asks,
    asked,
    index_v,
    index_s,
    rows_of,
    lanes_of,
    best,
    part,
    parts,
    last,
    code_sem,
    local_sem,
    z_send,
    z_recv,
    ask_send,
    ask_recv,
    near_send,
    near_recv,
    relay_send,
    far_recv,
    fwd_send,
    fwd_recv,
    part_send,
    part_recv,
    last_send,
    last_recv,
):
    shard = lax.axis_index("corpus")
    member = lax.axis_index("cent")
    core = member % 2
    chip = member // 2
    partner = chip * 2 + (1 - core)
    chip_x, chip_y = chip // 4, chip % 4
    mine = core * 128 + chip * GROUPS

    def peer(step):
        return lax.rem(member + step, MEMBERS)

    def other(step):
        return lax.rem(shard + step, GROUPS)

    def local(src, dst, n):
        return pltpu.make_async_copy(src, dst, local_sem.at[n])

    own_query = local(q_hbm, queries.at[mine], 0)
    own_query.start()
    barrier = pltpu.get_barrier_semaphore()
    each(
        1,
        GROUPS,
        lambda s: pl.semaphore_signal(
            barrier, inc=1, device_id=(other(s), member), device_id_type=MESH
        ),
    )
    each(
        1,
        MEMBERS,
        lambda s: pl.semaphore_signal(
            barrier, inc=1, device_id=(shard, peer(s)), device_id_type=MESH
        ),
    )

    fetches = [
        local(cand_hbm, cand_ref, 1),
        local(table_hbm, table_ref, 2),
        local(len_hbm, len_ref, 3),
        local(tok_hbm, tok_v, 4),
        local(bw_hbm, bw_ref, 5),
        local(cent_hbm, cent, 6),
    ]
    for fetch in fetches:
        fetch.start()

    def code_copy(p):
        return pltpu.make_async_copy(codes_hbm.at[p], codes.at[p], code_sem.at[p])

    each(0, PASSAGES, lambda p: code_copy(p).start())

    def widen(i):
        s = pl.ds(pl.multiple_of(i * 256, 256), 256)
        table32[s, :] = cent[s, :].astype(F32)

    def gather(p, rows, start, size):
        ids = tok_ref.at[p]
        for s in range(start, start + size):
            rows[pl.ds(s, 1), :] = table32[pl.ds(ids[s], 1), :]

    def finish(p, rows, s0, top):
        w0, w1, w2, w3 = bw_ref[0], bw_ref[1], bw_ref[2], bw_ref[3]
        c = codes[p, pl.ds(s0, 32), :]
        r = jnp.where(c < 2, jnp.where(c == 0, w0, w1), jnp.where(c == 2, w2, w3))
        x = rows[pl.ds(s0, 32), :] + r
        y = x * lax.rsqrt(jnp.sum(x * x, axis=-1, keepdims=True) + 1e-6)
        if s0 == 0:
            top = jnp.broadcast_to(y[0:1, :], (32, DIM))
        y = jnp.where(iota((32, DIM), 0) + s0 < len_ref[0, p], y, top)
        embed[p, pl.ds(s0, 32), :] = y.astype(BF16)
        return top

    def decode(pair):
        p = 2 * pair
        later = jnp.minimum(p + 2, PASSAGES - 1)
        code_copy(p).wait()
        code_copy(p + 1).wait()
        for now, this, nxt, that in ((p, rows_a, p + 1, rows_b), (p + 1, rows_b, later, rows_a)):
            top = None
            for s0 in range(0, PT, 32):
                gather(nxt, that, s0, 32)
                top = finish(now, this, s0, top)

    def z_copy(step):
        return pltpu.make_async_remote_copy(
            src_ref=queries.at[mine],
            dst_ref=queries.at[mine + order(step)],
            send_sem=z_send.at[step - 1],
            recv_sem=z_recv.at[step - 1],
            device_id=(other(step), member),
            device_id_type=MESH,
        )

    def moved(axis, d):
        return lax.rem(chip_x + d * (1 - axis), 4) * 4 + lax.rem(chip_y + d * axis, 4)

    def near_copy(axis, d, half):
        block = queries.at[pl.ds(mine + 4 * half, 4)]
        return pltpu.make_async_remote_copy(
            src_ref=block,
            dst_ref=block,
            send_sem=near_send.at[axis, d, half],
            recv_sem=near_recv.at[axis, d, half],
            device_id=(shard, moved(axis, d) * 2 + core),
            device_id_type=MESH,
        )

    def relay_copy(half, d, e):
        source = moved(half, 4 - d)
        block = queries.at[pl.ds(core * 128 + source * GROUPS + 4 * half, 4)]
        return pltpu.make_async_remote_copy(
            src_ref=block,
            dst_ref=block,
            send_sem=relay_send.at[half, d, e],
            recv_sem=far_recv.at[d * (1 - half) + e * half, d * half + e * (1 - half)],
            device_id=(shard, moved(1 - half, e) * 2 + core),
            device_id_type=MESH,
        )

    def source_block(dx, dy):
        source = lax.rem(chip_x + 4 - dx, 4) * 4 + lax.rem(chip_y + 4 - dy, 4)
        return queries.at[pl.ds(core * 128 + source * GROUPS, GROUPS)]

    def exchanged(src, dst, send, recv, count):
        pltpu.make_async_remote_copy(
            src_ref=src.at[pl.ds(0, count)],
            dst_ref=dst.at[pl.ds(0, count)],
            send_sem=send,
            recv_sem=recv,
            device_id=(shard, partner),
            device_id_type=MESH,
        ).wait()

    def fwd_copy(dx, dy):
        block = source_block(dx, dy)
        return pltpu.make_async_remote_copy(
            src_ref=block,
            dst_ref=block,
            send_sem=fwd_send.at[dx, dy],
            recv_sem=fwd_recv.at[dx, dy],
            device_id=(shard, partner),
            device_id_type=MESH,
        )

    def far_wait(dx, dy):
        block = source_block(dx, dy)
        pltpu.make_async_remote_copy(
            src_ref=block,
            dst_ref=block,
            send_sem=fwd_send.at[dx, dy],
            recv_sem=far_recv.at[dx, dy],
            device_id=(shard, partner),
            device_id_type=MESH,
        ).wait_recv()

    def ask_copy(step):
        return pltpu.make_async_remote_copy(
            src_ref=asks.at[peer(step)],
            dst_ref=asked.at[member],
            send_sem=ask_send,
            recv_sem=ask_recv,
            device_id=(shard, peer(step)),
            device_id_type=MESH,
        )

    def send_near(half):
        for axis in range(2):
            each(1, 4, lambda d: near_copy(axis, d, half).start())

    def relay(half):
        def one(d):
            near_copy(half, d, half).wait_recv()
            each(1, 4, lambda e: relay_copy(half, d, e).start())

        each(1, 4, one)

    own_query.wait()
    pl.semaphore_wait(barrier, MEMBERS + GROUPS - 2)
    each(1, GROUPS, lambda s: z_copy(s).start())
    for fetch in fetches[:2]:
        fetch.wait()
    tiles = request_tiles(cand_ref[...], table_ref[...], member)
    row = iota((8, 128), 0) == member // 8
    for m in range(MEMBERS):
        asks[m] = jnp.where(row, jnp.broadcast_to(tiles[m : m + 1, :], (8, 128)), 0)
    each(1, MEMBERS, lambda s: ask_copy(s).start())
    fetches[3].wait()
    tok_v[...] = tok_v[...] & (CENTS - 1)
    ids_copy = local(tok_v, tok_ref, 4)
    ids_copy.start()
    for fetch in fetches[2:3] + fetches[4:]:
        fetch.wait()
    each(0, CENTS // 256, widen)
    ids_copy.wait()
    gather(0, rows_a, 0, PT)

    each(0, FIRST, decode)
    for step in (1, 7, 2):
        z_copy(step).wait_recv()
    send_near(0)
    done = FIRST + SECOND
    each(FIRST, done, decode)
    for step in (6, 3, 5, 4):
        z_copy(step).wait_recv()
    send_near(1)
    fwd_copy(0, 0).start()
    each(done, done + THIRD, decode)
    done = done + THIRD
    relay(0)
    each(done, done + FOURTH, decode)
    done = done + FOURTH
    relay(1)
    each(done, PASSAGES // 2, decode)

    asked[member] = asks[member]
    exchanged(asks, asked, ask_send, ask_recv, MEMBERS - 1)
    packed = asked[0]
    for m in range(1, MEMBERS):
        packed = packed + asked[m]
    index, srow, slane = chunk_tables(packed, shard)
    index_v[...] = index
    index_copy = local(index_v, index_s, 0)
    index_copy.start()
    for j in range(WIDE):
        lane = slice(128 * j, 128 * (j + 1))
        rows_of[:, lane] = one_hot(iota((64, 128), 0) + 1 == srow[j : j + 1, :]).astype(BF16)
        lanes_of[:, lane] = one_hot(iota((128, 128), 0) == slane[j : j + 1, :]).astype(BF16)

    each(1, 4, lambda d: near_copy(1, d, 0).wait_recv())
    each(1, 4, lambda d: near_copy(0, d, 1).wait_recv())
    each(1, 4, lambda d: fwd_copy(d, 0).start())
    each(1, 4, lambda d: fwd_copy(0, d).start())

    def far_on(n):
        dx, dy = n // 3 + 1, n % 3 + 1
        far_wait(dx, dy)
        fwd_copy(dx, dy).start()

    each(0, 9, far_on)
    index_copy.wait()
    each(1, GROUPS, lambda s: z_copy(s).wait_send())

    def near_sent(n):
        for axis in range(2):
            near_copy(axis, n // 2 + 1, n % 2).wait_send()

    def relays_sent(n):
        for half in range(2):
            relay_copy(half, n // 3 + 1, n % 3 + 1).wait_send()

    each(0, 16, lambda n: fwd_copy(n // 4, n % 4).wait())

    best[pl.ds(CHUNKS, 128 - CHUNKS), :] = jnp.zeros((128 - CHUNKS, WIDE * QT), F32)

    def score(b):
        for v in range(DEEP):
            found = []
            for u in range(8):
                ch = (b * DEEP + v) * 8 + u
                e = embed[index_s[8, ch] & (PASSAGES - 1)]
                q = jnp.concatenate(
                    [queries[index_s[j, ch] & 255] for j in range(WIDE)], axis=0
                )
                dots = lax.dot_general(e, q, NT, preferred_element_type=F32)
                found.append(jnp.max(dots, axis=0, keepdims=True))
            start = pl.multiple_of((b * DEEP + v) * 8, 8)
            best[pl.ds(start, 8), :] = jnp.concatenate(found, axis=0)

    each(0, CHUNKS // 8 // DEEP, score)

    gather32 = one_hot(iota((WIDE, WIDE * QT), 1) // QT == iota((WIDE, WIDE * QT), 0))
    gather32 = gather32.astype(BF16)

    def thirds(x):
        a = x.astype(BF16)
        b = (x - a.astype(F32)).astype(BF16)
        c = (x - a.astype(F32) - b.astype(F32)).astype(BF16)
        return a, b, c

    total = jnp.zeros((WIDE, 128), F32)
    for piece in thirds(best[...]):
        total = total + lax.dot_general(gather32, piece, NT, preferred_element_type=F32)
    left = []
    for piece in thirds(total):
        left.append(
            jnp.concatenate(
                [
                    rows_of[:, 128 * j : 128 * (j + 1)]
                    * jnp.broadcast_to(piece[j : j + 1, :], (64, 128))
                    for j in range(WIDE)
                ],
                axis=1,
            )
        )
    table = lax.dot_general(
        jnp.concatenate(left, axis=0), lanes_of[...], NT, preferred_element_type=F32
    )
    table = table[0:64] + table[64:128] + table[128:192]
    for m in range(MEMBERS):
        part[m] = table[2 * m : 2 * m + 2, :]

    def part_copy(step):
        return pltpu.make_async_remote_copy(
            src_ref=part.at[peer(step)],
            dst_ref=parts.at[member],
            send_sem=part_send,
            recv_sem=part_recv,
            device_id=(shard, peer(step)),
            device_id_type=MESH,
        )

    for step in FARTHEST_MEMBERS:
        part_copy(step).start()
    parts[member] = part[member]
    each(0, 6, near_sent)
    each(0, 9, relays_sent)
    exchanged(part, parts, part_send, part_recv, MEMBERS - 1)
    tot = parts[0]
    for m in range(1, MEMBERS):
        tot = tot + parts[m]

    quarter = iota((8, 128), 1) // K == shard % 4
    row_in = iota((2, 128), 0) == shard // 4
    for o in range(GROUPS):
        line = jnp.broadcast_to(tot[o // 4 : o // 4 + 1, :], (8, 128))
        shift = lax.rem(shard + 4 - o % 4, 4) * K
        line = jnp.where(quarter, pltpu.roll(line, shift, 1), 0.0)
        last[o] = jnp.where(row_in, line[0:2, :], 0.0)

    def last_copy(step):
        return pltpu.make_async_remote_copy(
            src_ref=last.at[other(step)],
            dst_ref=lasts.at[shard],
            send_sem=last_send,
            recv_sem=last_recv,
            device_id=(other(step), member),
            device_id_type=MESH,
        )

    for step in FARTHEST_SHARDS:
        last_copy(step).start()
    own_last = local(last.at[shard], lasts.at[shard], 0)
    own_last.start()
    own_last.wait()
    exchanged(last, lasts, last_send, last_recv, GROUPS - 1)


def body(
    queries,
    candidates,
    storage_row,
    lengths,
    token_cents,
    residual_codes,
    centroids,
    bucket_weights,
):
    hbm = pl.BlockSpec(memory_space=pl.ANY)
    dma = pltpu.SemaphoreType.DMA
    out = pl.pallas_call(
        kernel,
        out_shape=jax.ShapeDtypeStruct((GROUPS, 2, 128), F32),
        in_specs=[hbm] * 8,
        out_specs=hbm,
        scratch_shapes=[
            pltpu.VMEM((GROUPS, K), I32),
            pltpu.VMEM((16, 128), I32),
            pltpu.SMEM((1, PASSAGES), I32),
            pltpu.VMEM((PASSAGES, PT), I32),
            pltpu.SMEM((PASSAGES, PT), I32),
            pltpu.SMEM((4,), F32),
            pltpu.VMEM((PASSAGES, PT, DIM), I32),
            pltpu.VMEM((CENTS, DIM), BF16),
            pltpu.VMEM((CENTS, DIM), F32),
            pltpu.VMEM((PT, DIM), F32),
            pltpu.VMEM((PT, DIM), F32),
            pltpu.VMEM((PASSAGES, PT, DIM), BF16),
            pltpu.VMEM((MEMBERS * GROUPS, QT, DIM), BF16),
            pltpu.VMEM((MEMBERS, 8, 128), I32),
            pltpu.VMEM((MEMBERS, 8, 128), I32),
            pltpu.VMEM((16, 128), I32),
            pltpu.SMEM((16, 128), I32),
            pltpu.VMEM((64, WIDE * 128), BF16),
            pltpu.VMEM((128, WIDE * 128), BF16),
            pltpu.VMEM((128, WIDE * QT), F32),
            pltpu.VMEM((MEMBERS, 2, 128), F32),
            pltpu.VMEM((MEMBERS, 2, 128), F32),
            pltpu.VMEM((GROUPS, 2, 128), F32),
            dma((PASSAGES,)),
            dma((7,)),
            dma((GROUPS - 1,)),
            dma((GROUPS - 1,)),
            dma,
            dma,
            dma((2, 4, 2)),
            dma((2, 4, 2)),
            dma((2, 4, 4)),
            dma((4, 4)),
            dma((4, 4)),
            dma((4, 4)),
            dma,
            dma,
            dma,
            dma,
        ],
        compiler_params=pltpu.CompilerParams(
            collective_id=0, has_side_effects=True, vmem_limit_bytes=67043328
        ),
    )(
        queries.reshape(QT, DIM),
        candidates.reshape(GROUPS, K),
        storage_row.reshape(16, 128),
        lengths,
        token_cents.reshape(PASSAGES, PT),
        residual_codes.reshape(PASSAGES, PT, DIM),
        centroids,
        bucket_weights,
    )
    return jnp.sum(out, axis=0).reshape(1, 1, GROUPS * K)


def solution(mesh):
    in_specs = (
        P("corpus", "cent", None, None),
        P("corpus", None, "cent", None),
        P("corpus", None),
        P("corpus", "cent"),
        P("corpus", "cent", None),
        P("corpus", "cent", None, None),
        P("cent", None),
        P(),
    )
    out_specs = P("corpus", "cent", None)
    return jax.shard_map(body, mesh=mesh, in_specs=in_specs, out_specs=out_specs, check_vma=False)
```

```python
import jax
import jax.numpy as jnp
from jax import lax
from jax.experimental import pallas as pl
from jax.experimental.pallas import tpu as pltpu
from jax.sharding import PartitionSpec as P

DIM = 128
QT = 32
PT = 128
GROUPS = 8
MEMBERS = 32
K = 32
ENTRIES = 256
CAP = 16
SLOTS = MEMBERS * CAP
PASSAGES = 64
CENTS = 8192
WIDE = 8
DEEP = 5
CHUNKS = 120
FIRST = 6
SECOND = 3
THIRD = 6
FOURTH = 4
MESH = pl.DeviceIdType.MESH


def ring(d, n):
    return min(d, n - d)


FARTHEST_MEMBERS = sorted(
    range(1, MEMBERS), key=lambda s: -ring(s // 8, 4) - ring(s // 2 % 4, 4)
)
FARTHEST_SHARDS = sorted(range(1, GROUPS), key=lambda s: -ring(s, GROUPS))
HIGH = lax.Precision.HIGHEST
NT = (((1,), (1,)), ((), ()))
F32, I32, BF16 = jnp.float32, jnp.int32, jnp.bfloat16


def iota(shape, dim):
    return lax.broadcasted_iota(I32, shape, dim)


def one_hot(flag):
    return jnp.where(flag, F32(1.0), F32(0.0))


def dot(a, b):
    return jnp.dot(a, b, preferred_element_type=F32)


def request_tiles(cand, table, member):
    lanes = iota((32, ENTRIES), 1)
    spread = one_hot(lanes % K == iota((32, ENTRIES), 0))
    wide = jnp.dot(cand.astype(F32), spread, precision=HIGH, preferred_element_type=F32)
    mine = iota((GROUPS, ENTRIES), 1) // K == iota((GROUPS, ENTRIES), 0)
    ident = jnp.sum(jnp.where(mine, wide, 0.0), axis=0, keepdims=True).astype(I32)
    low = one_hot(iota((128, ENTRIES), 0) == (ident & 127))
    looked = jnp.dot(table.astype(F32), low, precision=HIGH, preferred_element_type=F32)
    high = iota((16, ENTRIES), 0) == (ident >> 7)
    row = jnp.sum(jnp.where(high, looked, 0.0), axis=0, keepdims=True).astype(I32)
    owner, stored = row >> 6, row & 63
    owned = one_hot(iota((MEMBERS, ENTRIES), 0) == owner)
    before = one_hot(iota((ENTRIES, ENTRIES), 0) < iota((ENTRIES, ENTRIES), 1))
    ahead = dot(owned.astype(BF16), before.astype(BF16))
    position = jnp.sum(owned * ahead, axis=0, keepdims=True).astype(I32)
    code = (stored * ENTRIES + iota((1, ENTRIES), 1) + 1).astype(F32)
    place = one_hot(iota((128, ENTRIES), 0) == position + (member % 8) * CAP)
    tiles = lax.dot_general(
        owned * code, place, NT, precision=HIGH, preferred_element_type=F32
    )
    return tiles.astype(I32)


def order(step):
    return jnp.where(step == 0, 0, jnp.where(step > 4, 2 * (GROUPS - step), 2 * step - 1))


def chunk_tables(packed, shard):
    code = jnp.concatenate([packed[r : r + 1, :] for r in range(4)], axis=1)
    there = code > 0
    stored = jnp.where(there, (code - 1) >> 8, PASSAGES)
    entry = jnp.where(there, (code - 1) & 255, 0)
    group, cand = entry >> 5, entry & 31
    source = iota((1, SLOTS), 1) >> 4
    kept = (source & 1) * 128 + (source >> 1) * GROUPS + order((shard + GROUPS - group) & 7)
    named = one_hot(iota((PASSAGES, SLOTS), 0) == stored)
    before = one_hot(iota((128, 128), 0) < iota((128, 128), 1)).astype(BF16)
    ones = jnp.ones((128, 128), BF16)
    ahead, count = [], jnp.zeros((PASSAGES, 128), F32)
    for r in range(4):
        piece = named[:, 128 * r : 128 * (r + 1)].astype(BF16)
        ahead.append(dot(piece, before) + count)
        count = count + dot(piece, ones)
    ahead = jnp.concatenate(ahead, axis=1)
    position = jnp.sum(named * ahead, axis=0, keepdims=True).astype(I32)
    needed = (count.astype(I32) + (WIDE - 1)) >> 3
    lower = one_hot(iota((PASSAGES, PASSAGES), 1) < iota((PASSAGES, PASSAGES), 0))
    first = dot(lower.astype(BF16), needed.astype(F32).astype(BF16))
    first4 = jnp.concatenate([first] * 4, axis=1)
    chunk = jnp.sum(named * first4, axis=0, keepdims=True).astype(I32) + (position >> 3)
    in_chunk = one_hot((iota((128, SLOTS), 0) == chunk) & there).astype(BF16)
    column = iota((WIDE, SLOTS), 0) == (position & 7)

    def placed(value):
        return jnp.where(column, value.astype(F32), 0.0)

    values = jnp.concatenate(
        [
            placed(kept),
            placed(source * 2 + (group >> 2) + 1),
            placed((group & 3) * K + cand),
        ],
        axis=0,
    ).astype(BF16)
    tables = lax.dot_general(values, in_chunk, NT, preferred_element_type=F32).astype(I32)
    ends = first.astype(I32) + needed
    passed = jnp.where(ends <= iota((PASSAGES, 128), 1), 1.0, 0.0)
    passage = jnp.sum(passed, axis=0, keepdims=True).astype(I32)
    passage = jnp.minimum(passage, PASSAGES - 1)
    index = jnp.concatenate(
        [tables[0:WIDE], jnp.broadcast_to(passage, (8, 128))], axis=0
    )
    return index, tables[8:16], tables[16:24]


def each(start, stop, step):
    def run(i, carry):
        step(i)
        return carry

    lax.fori_loop(start, stop, run, 0)


def kernel(
    q_hbm,
    cand_hbm,
    table_hbm,
    len_hbm,
    tok_hbm,
    codes_hbm,
    cent_hbm,
    bw_hbm,
    lasts,
    cand_ref,
    table_ref,
    len_ref,
    tok_v,
    tok_ref,
    bw_ref,
    codes,
    cent,
    table32,
    rows_a,
    rows_b,
    embed,
    queries,
    asks,
    asked,
    index_v,
    index_s,
    rows_of,
    lanes_of,
    best,
    part,
    parts,
    last,
    code_sem,
    local_sem,
    z_send,
    z_recv,
    ask_send,
    ask_recv,
    near_send,
    near_recv,
    relay_send,
    far_recv,
    fwd_send,
    fwd_recv,
    part_send,
    part_recv,
    last_send,
    last_recv,
):
    shard = lax.axis_index("corpus")
    member = lax.axis_index("cent")
    core = member % 2
    chip = member // 2
    partner = chip * 2 + (1 - core)
    chip_x, chip_y = chip // 4, chip % 4
    mine = core * 128 + chip * GROUPS

    def peer(step):
        return lax.rem(member + step, MEMBERS)

    def other(step):
        return lax.rem(shard + step, GROUPS)

    def local(src, dst, n):
        return pltpu.make_async_copy(src, dst, local_sem.at[n])

    own_query = local(q_hbm, queries.at[mine], 0)
    own_query.start()
    barrier = pltpu.get_barrier_semaphore()
    each(
        1,
        GROUPS,
        lambda s: pl.semaphore_signal(
            barrier, inc=1, device_id=(other(s), member), device_id_type=MESH
        ),
    )
    each(
        1,
        MEMBERS,
        lambda s: pl.semaphore_signal(
            barrier, inc=1, device_id=(shard, peer(s)), device_id_type=MESH
        ),
    )

    fetches = [
        local(cand_hbm, cand_ref, 1),
        local(table_hbm, table_ref, 2),
        local(len_hbm, len_ref, 3),
        local(tok_hbm, tok_v, 4),
        local(bw_hbm, bw_ref, 5),
        local(cent_hbm, cent, 6),
    ]
    for fetch in fetches:
        fetch.start()

    def code_copy(p):
        return pltpu.make_async_copy(codes_hbm.at[p], codes.at[p], code_sem.at[p])

    each(0, PASSAGES, lambda p: code_copy(p).start())

    def widen(i):
        s = pl.ds(pl.multiple_of(i * 256, 256), 256)
        table32[s, :] = cent[s, :].astype(F32)

    def gather(p, rows, start, size):
        ids = tok_ref.at[p]
        for s in range(start, start + size):
            rows[pl.ds(s, 1), :] = table32[pl.ds(ids[s], 1), :]

    def finish(p, rows, s0, top):
        w0, w1, w2, w3 = bw_ref[0], bw_ref[1], bw_ref[2], bw_ref[3]
        c = codes[p, pl.ds(s0, 32), :]
        r = jnp.where(c < 2, jnp.where(c == 0, w0, w1), jnp.where(c == 2, w2, w3))
        x = rows[pl.ds(s0, 32), :] + r
        y = x * lax.rsqrt(jnp.sum(x * x, axis=-1, keepdims=True) + 1e-6)
        if s0 == 0:
            top = jnp.broadcast_to(y[0:1, :], (32, DIM))
        y = jnp.where(iota((32, DIM), 0) + s0 < len_ref[0, p], y, top)
        embed[p, pl.ds(s0, 32), :] = y.astype(BF16)
        return top

    def decode(pair):
        p = 2 * pair
        later = jnp.minimum(p + 2, PASSAGES - 1)
        code_copy(p).wait()
        code_copy(p + 1).wait()
        for now, this, nxt, that in ((p, rows_a, p + 1, rows_b), (p + 1, rows_b, later, rows_a)):
            top = None
            for s0 in range(0, PT, 32):
                gather(nxt, that, s0, 32)
                top = finish(now, this, s0, top)

    def z_copy(step):
        return pltpu.make_async_remote_copy(
            src_ref=queries.at[mine],
            dst_ref=queries.at[mine + order(step)],
            send_sem=z_send.at[step - 1],
            recv_sem=z_recv.at[step - 1],
            device_id=(other(step), member),
            device_id_type=MESH,
        )

    def moved(axis, d):
        return lax.rem(chip_x + d * (1 - axis), 4) * 4 + lax.rem(chip_y + d * axis, 4)

    def near_copy(axis, d, half):
        block = queries.at[pl.ds(mine + 4 * half, 4)]
        return pltpu.make_async_remote_copy(
            src_ref=block,
            dst_ref=block,
            send_sem=near_send.at[axis, d, half],
            recv_sem=near_recv.at[axis, d, half],
            device_id=(shard, moved(axis, d) * 2 + core),
            device_id_type=MESH,
        )

    def relay_copy(half, d, e):
        source = moved(half, 4 - d)
        block = queries.at[pl.ds(core * 128 + source * GROUPS + 4 * half, 4)]
        return pltpu.make_async_remote_copy(
            src_ref=block,
            dst_ref=block,
            send_sem=relay_send.at[half, d, e],
            recv_sem=far_recv.at[d * (1 - half) + e * half, d * half + e * (1 - half)],
            device_id=(shard, moved(1 - half, e) * 2 + core),
            device_id_type=MESH,
        )

    def source_block(dx, dy):
        source = lax.rem(chip_x + 4 - dx, 4) * 4 + lax.rem(chip_y + 4 - dy, 4)
        return queries.at[pl.ds(core * 128 + source * GROUPS, GROUPS)]

    def exchanged(src, dst, send, recv, count):
        pltpu.make_async_remote_copy(
            src_ref=src.at[pl.ds(0, count)],
            dst_ref=dst.at[pl.ds(0, count)],
            send_sem=send,
            recv_sem=recv,
            device_id=(shard, partner),
            device_id_type=MESH,
        ).wait()

    def fwd_copy(dx, dy):
        block = source_block(dx, dy)
        return pltpu.make_async_remote_copy(
            src_ref=block,
            dst_ref=block,
            send_sem=fwd_send.at[dx, dy],
            recv_sem=fwd_recv.at[dx, dy],
            device_id=(shard, partner),
            device_id_type=MESH,
        )

    def far_wait(dx, dy):
        block = source_block(dx, dy)
        pltpu.make_async_remote_copy(
            src_ref=block,
            dst_ref=block,
            send_sem=fwd_send.at[dx, dy],
            recv_sem=far_recv.at[dx, dy],
            device_id=(shard, partner),
            device_id_type=MESH,
        ).wait_recv()

    def ask_copy(step):
        return pltpu.make_async_remote_copy(
            src_ref=asks.at[peer(step)],
            dst_ref=asked.at[member],
            send_sem=ask_send,
            recv_sem=ask_recv,
            device_id=(shard, peer(step)),
            device_id_type=MESH,
        )

    def send_near(half):
        for axis in range(2):
            each(1, 4, lambda d: near_copy(axis, d, half).start())

    def relay(half):
        def one(d):
            near_copy(half, d, half).wait_recv()
            each(1, 4, lambda e: relay_copy(half, d, e).start())

        each(1, 4, one)

    own_query.wait()
    pl.semaphore_wait(barrier, MEMBERS + GROUPS - 2)
    each(1, GROUPS, lambda s: z_copy(s).start())
    for fetch in fetches[:2]:
        fetch.wait()
    tiles = request_tiles(cand_ref[...], table_ref[...], member)
    row = iota((8, 128), 0) == member // 8
    for m in range(MEMBERS):
        asks[m] = jnp.where(row, jnp.broadcast_to(tiles[m : m + 1, :], (8, 128)), 0)
    each(1, MEMBERS, lambda s: ask_copy(s).start())
    fetches[3].wait()
    tok_v[...] = tok_v[...] & (CENTS - 1)
    ids_copy = local(tok_v, tok_ref, 4)
    ids_copy.start()
    for fetch in fetches[2:3] + fetches[4:]:
        fetch.wait()
    each(0, CENTS // 256, widen)
    ids_copy.wait()
    gather(0, rows_a, 0, PT)

    each(0, FIRST, decode)
    for step in (1, 7, 2):
        z_copy(step).wait_recv()
    send_near(0)
    done = FIRST + SECOND
    each(FIRST, done, decode)
    for step in (6, 3, 5, 4):
        z_copy(step).wait_recv()
    send_near(1)
    fwd_copy(0, 0).start()
    each(done, done + THIRD, decode)
    done = done + THIRD
    relay(0)
    each(done, done + FOURTH, decode)
    done = done + FOURTH
    relay(1)
    each(1, 4, lambda d: near_copy(1, d, 0).wait_recv())
    each(1, 4, lambda d: near_copy(0, d, 1).wait_recv())
    each(1, 4, lambda d: fwd_copy(d, 0).start())
    each(1, 4, lambda d: fwd_copy(0, d).start())
    each(done, PASSAGES // 2, decode)

    asked[member] = asks[member]
    exchanged(asks, asked, ask_send, ask_recv, MEMBERS - 1)
    packed = asked[0]
    for m in range(1, MEMBERS):
        packed = packed + asked[m]
    index, srow, slane = chunk_tables(packed, shard)
    index_v[...] = index
    index_copy = local(index_v, index_s, 0)
    index_copy.start()
    for j in range(WIDE):
        lane = slice(128 * j, 128 * (j + 1))
        rows_of[:, lane] = one_hot(iota((64, 128), 0) + 1 == srow[j : j + 1, :]).astype(BF16)
        lanes_of[:, lane] = one_hot(iota((128, 128), 0) == slane[j : j + 1, :]).astype(BF16)

    def far_on(n):
        dx, dy = n // 3 + 1, n % 3 + 1
        far_wait(dx, dy)
        fwd_copy(dx, dy).start()

    each(0, 9, far_on)
    index_copy.wait()
    each(1, GROUPS, lambda s: z_copy(s).wait_send())

    def near_sent(n):
        for axis in range(2):
            near_copy(axis, n // 2 + 1, n % 2).wait_send()

    def relays_sent(n):
        for half in range(2):
            relay_copy(half, n // 3 + 1, n % 3 + 1).wait_send()

    each(0, 16, lambda n: fwd_copy(n // 4, n % 4).wait())

    best[pl.ds(CHUNKS, 128 - CHUNKS), :] = jnp.zeros((128 - CHUNKS, WIDE * QT), F32)

    def score(b):
        for v in range(DEEP):
            found = []
            for u in range(8):
                ch = (b * DEEP + v) * 8 + u
                e = embed[index_s[8, ch] & (PASSAGES - 1)]
                q = jnp.concatenate(
                    [queries[index_s[j, ch] & 255] for j in range(WIDE)], axis=0
                )
                dots = lax.dot_general(e, q, NT, preferred_element_type=F32)
                found.append(jnp.max(dots, axis=0, keepdims=True))
            start = pl.multiple_of((b * DEEP + v) * 8, 8)
            best[pl.ds(start, 8), :] = jnp.concatenate(found, axis=0)

    each(0, CHUNKS // 8 // DEEP, score)

    gather32 = one_hot(iota((WIDE, WIDE * QT), 1) // QT == iota((WIDE, WIDE * QT), 0))
    gather32 = gather32.astype(BF16)

    def thirds(x):
        a = x.astype(BF16)
        b = (x - a.astype(F32)).astype(BF16)
        c = (x - a.astype(F32) - b.astype(F32)).astype(BF16)
        return a, b, c

    total = jnp.zeros((WIDE, 128), F32)
    for piece in thirds(best[...]):
        total = total + lax.dot_general(gather32, piece, NT, preferred_element_type=F32)
    left = []
    for piece in thirds(total):
        left.append(
            jnp.concatenate(
                [
                    rows_of[:, 128 * j : 128 * (j + 1)]
                    * jnp.broadcast_to(piece[j : j + 1, :], (64, 128))
                    for j in range(WIDE)
                ],
                axis=1,
            )
        )
    table = lax.dot_general(
        jnp.concatenate(left, axis=0), lanes_of[...], NT, preferred_element_type=F32
    )
    table = table[0:64] + table[64:128] + table[128:192]
    for m in range(MEMBERS):
        part[m] = table[2 * m : 2 * m + 2, :]

    def part_copy(step):
        return pltpu.make_async_remote_copy(
            src_ref=part.at[peer(step)],
            dst_ref=parts.at[member],
            send_sem=part_send,
            recv_sem=part_recv,
            device_id=(shard, peer(step)),
            device_id_type=MESH,
        )

    for step in FARTHEST_MEMBERS:
        part_copy(step).start()
    parts[member] = part[member]
    each(0, 6, near_sent)
    each(0, 9, relays_sent)
    exchanged(part, parts, part_send, part_recv, MEMBERS - 1)
    tot = parts[0]
    for m in range(1, MEMBERS):
        tot = tot + parts[m]

    quarter = iota((8, 128), 1) // K == shard % 4
    row_in = iota((2, 128), 0) == shard // 4
    for o in range(GROUPS):
        line = jnp.broadcast_to(tot[o // 4 : o // 4 + 1, :], (8, 128))
        shift = lax.rem(shard + 4 - o % 4, 4) * K
        line = jnp.where(quarter, pltpu.roll(line, shift, 1), 0.0)
        last[o] = jnp.where(row_in, line[0:2, :], 0.0)

    def last_copy(step):
        return pltpu.make_async_remote_copy(
            src_ref=last.at[other(step)],
            dst_ref=lasts.at[shard],
            send_sem=last_send,
            recv_sem=last_recv,
            device_id=(other(step), member),
            device_id_type=MESH,
        )

    for step in FARTHEST_SHARDS:
        last_copy(step).start()
    own_last = local(last.at[shard], lasts.at[shard], 0)
    own_last.start()
    own_last.wait()
    exchanged(last, lasts, last_send, last_recv, GROUPS - 1)


def body(
    queries,
    candidates,
    storage_row,
    lengths,
    token_cents,
    residual_codes,
    centroids,
    bucket_weights,
):
    hbm = pl.BlockSpec(memory_space=pl.ANY)
    dma = pltpu.SemaphoreType.DMA
    out = pl.pallas_call(
        kernel,
        out_shape=jax.ShapeDtypeStruct((GROUPS, 2, 128), F32),
        in_specs=[hbm] * 8,
        out_specs=hbm,
        scratch_shapes=[
            pltpu.VMEM((GROUPS, K), I32),
            pltpu.VMEM((16, 128), I32),
            pltpu.SMEM((1, PASSAGES), I32),
            pltpu.VMEM((PASSAGES, PT), I32),
            pltpu.SMEM((PASSAGES, PT), I32),
            pltpu.SMEM((4,), F32),
            pltpu.VMEM((PASSAGES, PT, DIM), I32),
            pltpu.VMEM((CENTS, DIM), BF16),
            pltpu.VMEM((CENTS, DIM), F32),
            pltpu.VMEM((PT, DIM), F32),
            pltpu.VMEM((PT, DIM), F32),
            pltpu.VMEM((PASSAGES, PT, DIM), BF16),
            pltpu.VMEM((MEMBERS * GROUPS, QT, DIM), BF16),
            pltpu.VMEM((MEMBERS, 8, 128), I32),
            pltpu.VMEM((MEMBERS, 8, 128), I32),
            pltpu.VMEM((16, 128), I32),
            pltpu.SMEM((16, 128), I32),
            pltpu.VMEM((64, WIDE * 128), BF16),
            pltpu.VMEM((128, WIDE * 128), BF16),
            pltpu.VMEM((128, WIDE * QT), F32),
            pltpu.VMEM((MEMBERS, 2, 128), F32),
            pltpu.VMEM((MEMBERS, 2, 128), F32),
            pltpu.VMEM((GROUPS, 2, 128), F32),
            dma((PASSAGES,)),
            dma((7,)),
            dma((GROUPS - 1,)),
            dma((GROUPS - 1,)),
            dma,
            dma,
            dma((2, 4, 2)),
            dma((2, 4, 2)),
            dma((2, 4, 4)),
            dma((4, 4)),
            dma((4, 4)),
            dma((4, 4)),
            dma,
            dma,
            dma,
            dma,
        ],
        compiler_params=pltpu.CompilerParams(
            collective_id=0, has_side_effects=True, vmem_limit_bytes=67043328
        ),
    )(
        queries.reshape(QT, DIM),
        candidates.reshape(GROUPS, K),
        storage_row.reshape(16, 128),
        lengths,
        token_cents.reshape(PASSAGES, PT),
        residual_codes.reshape(PASSAGES, PT, DIM),
        centroids,
        bucket_weights,
    )
    return jnp.sum(out, axis=0).reshape(1, 1, GROUPS * K)


def solution(mesh):
    in_specs = (
        P("corpus", "cent", None, None),
        P("corpus", None, "cent", None),
        P("corpus", None),
        P("corpus", "cent"),
        P("corpus", "cent", None),
        P("corpus", "cent", None, None),
        P("cent", None),
        P(),
    )
    out_specs = P("corpus", "cent", None)
    return jax.shard_map(body, mesh=mesh, in_specs=in_specs, out_specs=out_specs, check_vma=False)
```
